256 devices in a mesh: apa: 16 (over z, core), slab: 4 (over x), band: 4 (over y).
Axes of the slice: x: 4, y: 4, z: 8, core: 2. Of those that a mesh axis runs over, the one named last changes fastest.
Arguments:
- raw: bfloat16 [32, 2560, 1024], P('apa', 'band', 'slab'), may hold values from -6 to 6
- dead_mask: int32 [32, 2560], P('apa', 'band'), may hold values 0 or 1
- kernel: bfloat16 [21, 257], replicated, may hold values from -0.078125 to 0.078125
- blob_wires: int32 [49152, 12], P(('apa', 'band')), may hold values from -1 to 81919, as said below
Outputs:
- signal: bfloat16 [32, 2560, 1024], P('apa', 'band', 'slab')
- blob_charge: float32 [49152, 512], P(('apa', 'band'), 'slab')
The draws below stay inside these ranges and needn't reach their ends.
Inputs may be any that keep to these rules, and one draw needn't show every extreme that they name: `blob_wires`: each entry is -1 or a wire a * 2560 + w of the whole detector. The owner of blob b is the device b // 768 in the order of apa+band. The wires named by one owner's blobs are distinct, and at most 128 of them are held by any one device (one band of its 2 APAs); in every draw some owner names exactly 128 from every such device.
All inputs are finite; a program needn't handle non-finite values. No bound on the sum of `dead_mask` on one device may be relied on, other than what follows from the above.
Results may differ from the reference program's by a relative error of at most 0.0051.
Values may be sent and summed in bfloat16 or wider, within the bound.
A program may use at most 128 MiB of HBM per device.

```python
import jax
import jax.numpy as jnp
from jax import lax

W = 2560
TICKS = 1024
WR = 10
H = 128
NI = 12
APA_DEV = 2
ROWS_PEER = 128
BLOB_DEV = 768
APAS = 32
BLOBS = 49152
SLICES = 512
N_APA = 16
N_BAND = 4


def draw_blob_wires(key, part):
    owners = N_APA * N_BAND
    per_owner = BLOB_DEV * NI
    band_wires = W // N_BAND
    source_rows = APA_DEV * band_wires
    key_busy, key_full, key_count, key_first, key_shuffle = jax.random.split(key, 5)
    busy_source = jax.random.randint(key_busy, (owners,), 0, 4) == 0
    counts = jax.random.randint(key_count, (owners, owners), 1, ROWS_PEER // 2 + 1)
    counts = jnp.where(busy_source[None, :], ROWS_PEER, counts)
    full_owner = jax.random.randint(key_full, (), 0, owners)
    counts = jnp.where(jnp.arange(owners)[:, None] == full_owner, ROWS_PEER, counts)
    first_row = jax.random.randint(key_first, (owners, owners), 0, source_rows - ROWS_PEER + 1)
    starts = jnp.cumsum(counts, axis=1) - counts
    totals = jnp.sum(counts, axis=1)
    owner_keys = jax.random.split(key_shuffle, owners)

    def one_owner(owner_key, start_row, first_rows, total):
        shuffle = jax.random.permutation(owner_key, per_owner)
        active = jnp.zeros((per_owner,), jnp.int32).at[shuffle].set((jnp.arange(per_owner) < total).astype(jnp.int32))
        position = jnp.cumsum(active) - 1
        source = jnp.sum((start_row[None, :] <= position[:, None]).astype(jnp.int32), axis=1) - 1
        source = jnp.clip(source, 0, owners - 1)
        src_row = first_rows[source] + position - start_row[source]
        src_row = jnp.clip(src_row, 0, source_rows - 1)
        apa_number = source // N_BAND * APA_DEV + src_row // band_wires
        wire_number = source % N_BAND * band_wires + src_row % band_wires
        return jnp.where(active > 0, apa_number * W + wire_number, -1)
    result = jax.vmap(one_owner)(owner_keys, starts, first_row, totals)
    return result.reshape(BLOBS, NI).astype(jnp.int32)


def touch_ends(values, key, low, top_value):
    shape = values.shape
    index_at = [jax.random.randint(jax.random.fold_in(key, axis), (), 0, shape[axis]) for axis in range(len(shape))]
    values = values.at[tuple(index_at)].set(low)
    longest = shape.index(max(shape))
    index_at[longest] = (index_at[longest] + 1) % shape[longest]
    return values.at[tuple(index_at)].set(top_value)


def levels(stream_key, shape, pieces, least, top_value):
    loudness = 1.0
    for dim, shards_of in pieces:
        heights = jax.random.uniform(jax.random.fold_in(jax.random.fold_in(stream_key, 6), dim), (shards_of,), jnp.float32, least / len(pieces), top_value / len(pieces))
        loudness = loudness * jnp.repeat(jnp.exp(heights), shape[dim] // shards_of).reshape((-1,) + (1,) * (len(shape) - 1 - dim))
    return loudness


def noise(own_key, extent, width, bound, pieces=(), held_as=jnp.bfloat16):
    factor_of = levels(own_key, extent, pieces, -0.22, 0.18) if pieces else 1.0
    drawn = jax.random.normal(own_key, extent, jnp.float32) * width * factor_of
    return jnp.minimum(jnp.maximum(drawn, -bound), bound).astype(held_as)


def setup_inputs(seed: int = 0) -> dict:
    keys = jax.random.split(jax.random.key(seed), 5)
    raw = noise(keys[0], (APAS, W, TICKS), 1.0, 6.0, ((0, 16), (1, 4), (2, 4)))
    dead_mask = touch_ends((jax.random.randint(keys[1], (APAS, W), 0, 8) < 7).astype(jnp.int32), jax.random.fold_in(keys[1], 1), 0, 1)
    kernel = noise(keys[2], (2 * WR + 1, 2 * H + 1), ((2 * WR + 1) * (2 * H + 1)) ** -0.5, 0.078125)
    blob_wires = draw_blob_wires(jax.random.fold_in(keys[4], 71), 0)
    return dict(raw=raw, dead_mask=dead_mask, kernel=kernel, blob_wires=blob_wires)


def reference(raw, dead_mask, kernel, blob_wires):
    holder = {"kernel": kernel}

    def one_apa(pair):
        wave, alive = pair
        clean = (wave * alive.astype(jnp.bfloat16)[:, None]).astype(jnp.float32)
        period = TICKS + 2 * H
        padded = jnp.pad(clean, ((WR, WR), (0, 2 * H)))
        wave_freq = jnp.fft.fft(padded, axis=1)
        weights = holder["kernel"].astype(jnp.float32)
        kernel_taps = jnp.zeros((2 * WR + 1, period), weights.dtype)
        kernel_taps = kernel_taps.at[:, :H + 1].set(weights[:, H:])
        kernel_taps = kernel_taps.at[:, period - H:].set(weights[:, :H])
        kernel_freq = jnp.fft.fft(kernel_taps, axis=1)
        total = kernel_freq[0][None, :] * wave_freq[0:W]
        for offset in range(1, 2 * WR + 1):
            total = total + kernel_freq[offset][None, :] * wave_freq[offset:offset + W]
        result = jnp.real(jnp.fft.ifft(total, axis=1))[:, :TICKS]
        return result.astype(jnp.bfloat16)

    signal = lax.map(one_apa, (raw, dead_mask))
    slice_charge = signal.astype(jnp.float32).reshape(APAS, W, SLICES, 2).sum(axis=3).astype(jnp.bfloat16)
    flat_rows = slice_charge.reshape(APAS * W, SLICES)
    blocks = blob_wires.reshape(BLOBS // BLOB_DEV, BLOB_DEV, NI)

    def one_owner(wires):
        usable = wires >= 0
        picked = flat_rows[jnp.where(usable, wires, 0)].astype(jnp.float32)
        return jnp.sum(jnp.where(usable[:, :, None], picked, jnp.zeros_like(picked)), axis=1)

    blob_charge = lax.map(one_owner, blocks).reshape(BLOBS, SLICES)
    return signal, blob_charge
```

```python
import math

import jax
import jax.numpy as jnp
from jax import lax
from jax.experimental import pallas as pl
from jax.experimental.pallas import tpu as pltpu
from jax.sharding import PartitionSpec as P

W = 2560
WR = 10
H = 128
ROWS_PEER = 128


def with_halo(block, sides, width):
    for axis, dim in sides:
        count = lax.axis_size(axis)
        forward = [(i, i + 1) for i in range(count - 1)]
        backward = [(target, source) for source, target in forward]
        low = lax.ppermute(
            lax.slice_in_dim(block, block.shape[dim] - width, None, axis=dim), axis, forward
        )
        high = lax.ppermute(lax.slice_in_dim(block, 0, width, axis=dim), axis, backward)
        block = jnp.concatenate([low, block, high], axis=dim)
    return block


def running_counts(hits):
    entries, groups = hits.shape
    block = math.gcd(entries, 128)
    blocks = entries // block
    stacked = hits.reshape(blocks, block, groups)
    inner_index = jnp.arange(block, dtype=jnp.int32)
    lower = (inner_index[:, None] >= inner_index[None, :]).astype(jnp.float32)
    inside = jnp.einsum(
        "ij,bjg->big",
        lower,
        stacked,
        precision=lax.Precision.HIGHEST,
        preferred_element_type=jnp.float32,
    )
    block_index = jnp.arange(blocks, dtype=jnp.int32)
    before = (block_index[:, None] > block_index[None, :]).astype(jnp.float32)
    offsets = jnp.dot(
        before,
        jnp.sum(stacked, axis=1),
        precision=lax.Precision.HIGHEST,
        preferred_element_type=jnp.float32,
    )
    return (inside + offsets[:, None, :]).reshape(entries, groups)


def tap_tables(kernel):
    offsets = 2 * WR + 1
    size = 2 * H

    def body(k_ref, out_ref, k32):
        k32[0:offsets, 0 : size + 1] = k_ref[...].astype(jnp.float32)
        source = lax.broadcasted_iota(jnp.int32, (size, size), 0)
        target = lax.broadcasted_iota(jnp.int32, (size, size), 1)

        def one(p, carry):
            row = k32[pl.ds(p, 1), 0:size]
            last = k32[pl.ds(p, 1), size : 2 * size][:, 0:1]
            taps = pltpu.roll(jnp.broadcast_to(row, (size, size)), 0, 1, stride=1, stride_axis=0)
            low = jnp.where(target < source, taps, jnp.where(target == source, last, 0.0))
            out_ref[p, 0:size, :] = low.astype(jnp.bfloat16)
            out_ref[p, size : 2 * size, :] = jnp.where(target >= source, taps, 0.0).astype(jnp.bfloat16)
            return carry

        lax.fori_loop(0, offsets, one, 0)

    return pl.pallas_call(
        body,
        out_shape=jax.ShapeDtypeStruct((offsets, 2 * size, size), jnp.bfloat16),
        in_specs=[pl.BlockSpec(memory_space=pltpu.VMEM)],
        out_specs=pl.BlockSpec(memory_space=pltpu.VMEM),
        scratch_shapes=[pltpu.VMEM((24, 2 * size), jnp.float32)],
        compiler_params=pltpu.CompilerParams(vmem_limit_bytes=24 << 20),
        cost_estimate=pl.CostEstimate(flops=0, bytes_accessed=6 << 20, transcendentals=0),
    )(kernel)


def shards(raw, dead_mask, kernel, blob_wires):
    apa_count, band_wires, slab_ticks = raw.shape
    length = slab_ticks + 2 * H
    clean = raw * dead_mask.astype(jnp.bfloat16)[:, :, None]
    extended = with_halo(clean, (("slab", 2),), H)
    widened = with_halo(extended, (("band", 1),), WR)
    tables = tap_tables(kernel)
    total = jnp.zeros((apa_count * band_wires, slab_ticks), jnp.float32)
    for offset in range(2 * WR + 1):
        shifted = widened[:, offset : offset + band_wires].reshape(apa_count * band_wires, length)
        total = total + jnp.dot(shifted, tables[offset], preferred_element_type=jnp.float32)
    signal = total.reshape(apa_count, band_wires, slab_ticks).astype(jnp.bfloat16)
    slice_count = slab_ticks // 2
    slice_rows = (
        signal.astype(jnp.float32).reshape(apa_count, band_wires, slice_count, 2).sum(axis=3)
    )
    slice_rows = slice_rows.astype(jnp.bfloat16).reshape(apa_count * band_wires, slice_count)
    apa_size = lax.axis_size("apa")
    band_count = lax.axis_size("band")
    groups = apa_size * band_count
    blob_count, places = blob_wires.shape
    wire_refs = blob_wires.reshape(-1)
    usable = wire_refs >= 0
    global_wire = jnp.where(usable, wire_refs, 0)
    apa_number = global_wire // W
    wire_number = global_wire % W
    source = apa_number // apa_count * band_count + wire_number // band_wires
    local_row = apa_number % apa_count * band_wires + wire_number % band_wires
    source_hot = (
        (source[:, None] == jnp.arange(groups, dtype=jnp.int32)[None, :]) & usable[:, None]
    ).astype(jnp.float32)
    counted = running_counts(source_hot)
    slot_index = jnp.sum(source_hot * (counted - 1.0), axis=1).astype(jnp.int32)
    slot_hot = (
        (slot_index[:, None] == jnp.arange(ROWS_PEER, dtype=jnp.int32)[None, :]) & usable[:, None]
    ).astype(jnp.float32)
    row_value = (local_row + 1).astype(jnp.float32)
    request = jnp.dot(
        (source_hot * row_value[:, None]).T,
        slot_hot,
        precision=lax.Precision.HIGHEST,
        preferred_element_type=jnp.float32,
    )
    request = request.astype(jnp.int32) - 1
    asked_rows = lax.all_to_all(request, ("apa", "band"), split_axis=0, concat_axis=0, tiled=True)
    held_rows = jnp.arange(apa_count * band_wires, dtype=jnp.int32)
    pick_table = (asked_rows[:, :, None] == held_rows[None, None, :]).astype(jnp.bfloat16)
    outgoing = jnp.einsum("gsr,rt->gst", pick_table, slice_rows, preferred_element_type=jnp.float32)
    outgoing = outgoing.astype(jnp.bfloat16)
    incoming = lax.all_to_all(outgoing, ("apa", "band"), split_axis=0, concat_axis=0, tiled=True)
    incoming = incoming.reshape(groups * ROWS_PEER, slice_count)
    placement = jnp.einsum(
        "bkg,bks->bgs",
        source_hot.reshape(blob_count, places, groups),
        slot_hot.reshape(blob_count, places, ROWS_PEER),
        precision=lax.Precision.HIGHEST,
        preferred_element_type=jnp.float32,
    )
    placement = placement.reshape(blob_count, groups * ROWS_PEER).astype(jnp.bfloat16)
    blob_charge = jnp.dot(placement, incoming, preferred_element_type=jnp.float32)
    return (signal, blob_charge)


def solution(mesh):
    return jax.shard_map(
        shards,
        mesh=mesh,
        in_specs=(P("apa", "band", "slab"), P("apa", "band"), P(), P(("apa", "band"), None)),
        out_specs=(P("apa", "band", "slab"), P(("apa", "band"), "slab")),
        check_vma=False,
    )
```

```python
import jax
import jax.numpy as jnp
from jax import lax
from jax.experimental import pallas as pl
from jax.experimental.pallas import tpu as pltpu
from jax.sharding import PartitionSpec as P

W = 2560
WR = 10
H = 128
TAPS = 2 * WR + 1
BANDS = 4
SLABS = 4
PLANES = 8
PEERS = 8
WIRES = W // BANDS
TICKS = 2 * H
LONG = 2 * TICKS
EDGE = 16
TALL = WIRES + 2 * EDGE
SLICES = TICKS // 2
SLOTS = 128
BLOBS = 768
PLACES = 12
COLS = 40
LANES = 128
BF = jnp.bfloat16
F32 = jnp.float32
MESH = pl.DeviceIdType.MESH


def iota(shape, dim):
    return lax.broadcasted_iota(jnp.int32, shape, dim)


def dot(a, b):
    return jnp.dot(a, b, preferred_element_type=F32)


def build_tables(k_ref, k32, tab):
    k32[...] = jnp.zeros_like(k32)
    k32[0:TAPS, 0 : TICKS + 1] = k_ref[...].astype(F32)
    source = iota((TICKS, TICKS), 0)
    target = iota((TICKS, TICKS), 1)

    def one(p, carry):
        row = k32[pl.ds(p, 1), 0:TICKS]
        last = k32[pl.ds(p, 1), TICKS:LONG][:, 0:1]
        taps = pltpu.roll(jnp.broadcast_to(row, (TICKS, TICKS)), 0, 1, stride=1, stride_axis=0)
        low = jnp.where(target < source, taps, jnp.where(target == source, last, 0.0))
        tab[p, 0:TICKS, :] = low.astype(BF)
        tab[p, TICKS:LONG, :] = jnp.where(target >= source, taps, 0.0).astype(BF)
        return carry

    lax.fori_loop(0, TAPS, one, 0)


def mask_waves(raw_ref, mask_ref, mask8, clean):
    mask8[...] = jnp.zeros_like(mask8)
    mask8[0:2, :] = mask_ref[...].astype(F32)
    live = jnp.transpose(mask8[...])
    for ap in range(2):
        wave = raw_ref[ap].astype(F32) * live[:, ap : ap + 1]
        clean[ap, EDGE : EDGE + WIRES, H : H + TICKS] = wave.astype(BF)


def interleave(clean, xf, xi, ap, has):
    left, right, above, below = has
    rows = ((0, EDGE, above), (EDGE, EDGE + WIRES, None), (EDGE + WIRES, TALL, below))
    cols = ((0, H, left), (H, H + TICKS, None), (H + TICKS, LONG, right))
    for r0, r1, row_ok in rows:
        for c0, c1, col_ok in cols:
            part = clean[ap, r0:r1, c0:c1].astype(F32)
            if row_ok is not None:
                part = jnp.where(row_ok, part, 0.0)
            if col_ok is not None:
                part = jnp.where(col_ok, part, 0.0)
            for t in range((c1 - c0) // LANES):
                xf[c0 // LANES + t, r0:r1, :] = part[:, t * LANES : (t + 1) * LANES]
    first = EDGE - WR

    def one(i, carry):
        for t in range(LONG // LANES):
            picked = xf[t, pl.ds(i + first, 16, stride=COLS), :]
            xi[ap, i, :, t * LANES : (t + 1) * LANES] = picked.astype(BF)
        return carry

    lax.fori_loop(0, COLS + 2 * WR, one, 0, unroll=4)


def convolve(xi, tab, so, sig_v, held, pair_sum, ap):
    tile = 20
    group = 7

    def one(n, carry):
        i0 = n * tile
        total = None
        for g in range(TAPS // group):
            parts = [
                xi[ap, pl.ds(i0 + g * group + q, tile)].reshape(tile * 16, LONG) for q in range(group)
            ]
            lhs = jnp.concatenate(parts, axis=1)
            rhs = tab[g * group : (g + 1) * group].reshape(group * LONG, TICKS)
            term = dot(lhs, rhs)
            total = term if total is None else total + term
        for i in range(tile):
            for t in range(TICKS // LANES):
                so[t, pl.ds(i0 + i, 16, stride=COLS), :] = total[
                    16 * i : 16 * (i + 1), t * LANES : (t + 1) * LANES
                ]
        return carry

    lax.fori_loop(0, COLS // tile, one, 0)
    wave = jnp.concatenate([so[t] for t in range(TICKS // LANES)], axis=1).astype(BF)
    sig_v[ap] = wave
    held[0, ap * WIRES : (ap + 1) * WIRES, :] = dot(wave, pair_sum).astype(BF)


def make_requests(wires_ref, request, bslot, packed, lower):
    refs = wires_ref[...]
    usable = refs >= 0
    wire = jnp.where(usable, refs, 0)
    apa = ((wire >> 9) * 205) >> 10
    wire = wire - apa * W
    band = ((wire >> 7) * 205) >> 10
    row = (apa & 1) * WIRES + wire - band * WIRES
    source = jnp.where(usable, (apa >> 1) * BANDS + band, 255)
    packed[...] = jnp.zeros_like(packed)
    packed[:, 0:PLACES] = source.astype(F32)
    packed[:, 16 : 16 + PLACES] = ((row >> 7) + 1).astype(F32)
    packed[:, 32 : 32 + PLACES] = (row & 127).astype(F32)
    entries = packed[...].astype(BF)
    spread_row = iota((LANES, 2 * LANES), 0)
    spread_col = iota((LANES, 2 * LANES), 1)
    base = jnp.where(spread_col < LANES, 0, jnp.where(spread_col < 192, 16, 32))
    lane = iota((BLOBS, LANES), 1)
    group_of = (lane & 63).astype(F32)
    slot_of = lane.astype(F32)
    blob = iota((BLOBS, LANES), 0)
    blob_value = jnp.where(lane < 64, (blob >> 7) + 1, blob & 127).astype(F32)
    block = BLOBS // 3
    lower[...] = (iota((block, block), 0) > iota((block, block), 1)).astype(F32).astype(BF)
    ones_top = (iota((LANES, LANES), 0) < 64).astype(F32).astype(BF)

    def one(k, carry):
        offset, total = carry
        spread = (spread_row == base + k).astype(F32).astype(BF)
        wide = dot(entries, spread)
        hot = (wide[:, 0:LANES] == group_of).astype(F32)
        hot16 = hot.astype(BF)
        ranks = []
        for j in range(3):
            piece = hot16[j * block : (j + 1) * block]
            inside = dot(lower[...], piece)
            ranks.append(inside + offset)
            offset = offset + inside[block - 1 : block] + hot[(j + 1) * block - 1 : (j + 1) * block]
        rank = jnp.concatenate(ranks, axis=0)
        slot = dot((hot * rank).astype(BF), ones_top)
        slot_hot = (slot == slot_of).astype(F32).astype(BF)
        values = jnp.concatenate(
            [(hot * wide[:, LANES:]).astype(BF), (hot * blob_value).astype(BF)], axis=1
        )
        found = lax.dot_general(
            slot_hot, values, (((0,), (0,)), ((), ())), preferred_element_type=F32
        )
        return offset, total + found

    _, table = lax.fori_loop(
        0, PLACES, one, (jnp.zeros((1, LANES), F32), jnp.zeros((SLOTS, 2 * LANES), F32))
    )
    request[...] = table[:, 0:LANES].astype(BF)
    high = table[:, LANES:]
    low = pltpu.roll(high, 64, 1)
    bslot[...] = jnp.transpose(high * 128.0 - 128.0 + low)


def pick(reqbox, held, picks, slot, plane, core, band):
    group = plane * 8 + core * BANDS + band
    place = iota((LANES, LANES), 0)
    choose = jnp.where(place == group, 128.0, jnp.where(place == group + 64, 1.0, 0.0)).astype(BF)
    lane = iota((2 * SLOTS, LANES), 1).astype(F32)

    def one(n, carry):
        asked = reqbox[pl.ds(2 * n, 2)].reshape(2 * SLOTS, LANES)
        row = dot(asked, choose)
        tiles = [
            (row == lane + 128.0 * (t + 1)).astype(F32).astype(BF) for t in range(2 * WIRES // LANES)
        ]
        got = dot(jnp.concatenate(tiles, axis=1), held[slot])
        picks[slot, pl.ds(2 * n, 2)] = got.astype(BF).reshape(2, SLOTS, SLICES)
        return carry

    lax.fori_loop(0, PEERS // 2, one, 0)


def place(bslot, picks, inbox, total, slot, plane, core, band):
    rows = []
    blocks = []
    for r in range(PEERS):
        dc, dy = divmod(r, BANDS)
        from_core = lax.rem(core + dc, 2)
        from_band = lax.rem(band + BANDS - dy, BANDS)
        rows.append(bslot[pl.ds(plane * 8 + from_core * BANDS + from_band, 1), :])
        blocks.append(picks[slot, 0] if r == 0 else inbox[slot, r])
    incoming = jnp.concatenate(blocks, axis=0)
    tile = 256
    blob = iota((tile, LANES), 0)

    def one(n, carry):
        index = (blob + n * tile).astype(F32)
        hot = jnp.concatenate([(index == row).astype(F32).astype(BF) for row in rows], axis=1)
        at = pl.ds(pl.multiple_of(n * tile, tile), tile)
        total[at, :] = total[at, :] + dot(hot, incoming)
        return carry

    lax.fori_loop(0, BLOBS // tile, one, 0)


def whole(
    raw_ref, mask_ref, k_ref, wires_ref, sig_ref, blob_ref,
    clean, xf, xi, tab, k32, mask8, so, sig_v, held, packed, lower, request, bslot,
    reqbox, picks, inbox,
    halo_send, halo_recv, req_send, req_recv, ring_send, ring_recv, box_send, box_recv, out_sem,
):
    apa = lax.axis_index("apa")
    slab = lax.axis_index("slab")
    band = lax.axis_index("band")
    plane = lax.div(apa, 2)
    core = lax.rem(apa, 2)

    def device(dz=0, dc=0, dx=0, dy=0):
        z = lax.rem(plane + dz + PLANES, PLANES)
        c = lax.rem(core + dc, 2)
        return (z * 2 + c, lax.rem(slab + dx + SLABS, SLABS), lax.rem(band + dy + BANDS, BANDS))

    peers = [device(dc=r // BANDS, dy=r % BANDS) for r in range(PEERS)]
    everyone = peers[1:] + [device(dz=1), device(dz=-1), device(dx=1), device(dx=-1)]
    everyone += [device(dx=i, dy=j) for i in (-1, 1) for j in (-1, 1)]
    barrier = pltpu.get_barrier_semaphore()
    for other in everyone:
        pl.semaphore_signal(barrier, inc=1, device_id=other, device_id_type=MESH)

    mask_waves(raw_ref, mask_ref, mask8, clean)
    pl.semaphore_wait(barrier, len(everyone))

    def remote(src, dst, send, recv, to):
        return pltpu.make_async_remote_copy(
            src_ref=src, dst_ref=dst, send_sem=send, recv_sem=recv, device_id=to, device_id_type=MESH
        )

    own = slice(EDGE, EDGE + WIRES)
    mid = slice(H, H + TICKS)
    row_parts = {
        -1: (slice(EDGE, 2 * EDGE), slice(EDGE + WIRES, TALL)),
        0: (own, own),
        1: (slice(WIRES, EDGE + WIRES), slice(0, EDGE)),
    }
    col_parts = {
        -1: (slice(H, 2 * H), slice(H + TICKS, LONG)),
        0: (mid, mid),
        1: (slice(2 * H, 3 * H), slice(0, H)),
    }
    halos = {0: [], 1: []}
    number = 0
    for ap in range(2):
        for dx in (-1, 0, 1):
            for dy in (-1, 0, 1):
                if dx == 0 and dy == 0:
                    continue
                (rs, rd), (cs, cd) = row_parts[dy], col_parts[dx]
                copy = remote(
                    clean.at[ap, rs, cs], clean.at[ap, rd, cd],
                    halo_send.at[number], halo_recv.at[number], device(dx=dx, dy=dy),
                )
                copy.start()
                halos[ap].append(copy)
                number += 1

    make_requests(wires_ref, request, bslot, packed, lower)
    reqbox[0] = request[...]
    asks = []
    for r in range(1, PEERS):
        dc, dy = divmod(r, BANDS)
        back = dc * BANDS + (BANDS - dy) % BANDS
        copy = remote(request, reqbox.at[back], req_send.at[back], req_recv.at[back], peers[r])
        copy.start()
        asks.append(copy)

    build_tables(k_ref, k32, tab)
    pair_sum = (iota((TICKS, SLICES), 0) >> 1) == iota((TICKS, SLICES), 1)
    pair_sum = pair_sum.astype(F32).astype(BF)
    has = (slab > 0, slab < SLABS - 1, band > 0, band < BANDS - 1)

    def half(ap):
        return slice(ap * WIRES, (ap + 1) * WIRES)

    towards = (device(dz=1), device(dz=-1))

    def slot_at(way, distance):
        if distance == 0:
            return 0
        if distance == 4:
            return 7
        return distance + 3 * way

    def ring(way, distance, ap):
        number = 2 * (distance - 1) + (ap if distance < 4 else 0)
        return remote(
            held.at[slot_at(way, distance - 1), half(ap)],
            held.at[slot_at(way, distance), half(ap)],
            ring_send.at[way, number], ring_recv.at[way, number], towards[way],
        )

    writes = []
    started = []
    for ap in range(2):
        for copy in halos[ap]:
            copy.wait_recv()
        interleave(clean, xf, xi, ap, has)
        convolve(xi, tab, so, sig_v, held, pair_sum, ap)
        for way in range(2):
            copy = ring(way, 1, ap)
            copy.start()
            started.append(copy)
        write = pltpu.make_async_copy(sig_v.at[ap], sig_ref.at[ap], out_sem.at[ap])
        write.start()
        writes.append(write)

    blob_ref[...] = jnp.zeros_like(blob_ref)
    for copy in asks:
        copy.wait_recv()
    boxes = {}

    def serve(slot, shift):
        source = lax.rem(plane + shift + PLANES, PLANES)
        pick(reqbox, held, picks, slot, source, core, band)
        boxes[slot] = []
        for r in range(1, PEERS):
            copy = remote(
                picks.at[slot, r], inbox.at[slot, r], box_send.at[slot, r], box_recv.at[slot, r], peers[r]
            )
            copy.start()
            boxes[slot].append(copy)

    def collect(slot, shift):
        source = lax.rem(plane + shift + PLANES, PLANES)
        for copy in boxes[slot]:
            copy.wait_recv()
        place(bslot, picks, inbox, blob_ref, slot, source, core, band)

    def forward(distance, ap):
        for way in range(2):
            ring(way, distance, ap).wait_recv()
            if distance < 3 or ap == way:
                copy = ring(way, distance + 1, ap)
                copy.start()
                started.append(copy)

    serve(0, 0)
    forward(1, 0)
    collect(0, 0)
    forward(1, 1)
    serve(1, -1)
    forward(2, 0)
    serve(4, 1)
    collect(1, -1)
    forward(2, 1)
    serve(2, -2)
    collect(4, 1)
    forward(3, 0)
    serve(5, 2)
    collect(2, -2)
    forward(3, 1)
    serve(3, -3)
    serve(6, 3)
    collect(5, 2)
    collect(3, -3)
    ring(0, 4, 0).wait_recv()
    ring(1, 4, 1).wait_recv()
    serve(7, 4)
    collect(6, 3)
    collect(7, 4)

    for copies in (halos[0], halos[1], asks, started, *boxes.values()):
        for copy in copies:
            copy.wait_send()
    for write in writes:
        write.wait()


def shards(raw, dead_mask, kernel, blob_wires):
    vmem = pl.BlockSpec(memory_space=pltpu.VMEM)
    dma = pltpu.SemaphoreType.DMA
    return pl.pallas_call(
        whole,
        out_shape=(
            jax.ShapeDtypeStruct((2, WIRES, TICKS), BF),
            jax.ShapeDtypeStruct((BLOBS, SLICES), F32),
        ),
        in_specs=[vmem] * 4,
        out_specs=(pl.BlockSpec(memory_space=pl.ANY), vmem),
        scratch_shapes=[
            pltpu.VMEM((2, TALL, LONG), BF),
            pltpu.VMEM((LONG // LANES, TALL, LANES), F32),
            pltpu.VMEM((2, COLS + 2 * WR, 16, LONG), BF),
            pltpu.VMEM((TAPS, LONG, TICKS), BF),
            pltpu.VMEM((24, LONG), F32),
            pltpu.VMEM((8, WIRES), F32),
            pltpu.VMEM((TICKS // LANES, WIRES, LANES), F32),
            pltpu.VMEM((2, WIRES, TICKS), BF),
            pltpu.VMEM((PLANES, 2 * WIRES, SLICES), BF),
            pltpu.VMEM((BLOBS, LANES), F32),
            pltpu.VMEM((BLOBS // 3, BLOBS // 3), BF),
            pltpu.VMEM((SLOTS, LANES), BF),
            pltpu.VMEM((LANES, SLOTS), F32),
            pltpu.VMEM((PEERS, SLOTS, LANES), BF),
            pltpu.VMEM((PLANES, PEERS, SLOTS, SLICES), BF),
            pltpu.VMEM((PLANES, PEERS, SLOTS, SLICES), BF),
            dma((16,)),
            dma((16,)),
            dma((PEERS,)),
            dma((PEERS,)),
            dma((2, 7)),
            dma((2, 7)),
            dma((PLANES, PEERS)),
            dma((PLANES, PEERS)),
            dma((2,)),
        ],
        compiler_params=pltpu.CompilerParams(
            collective_id=0, has_side_effects=True, vmem_limit_bytes=56 << 20
        ),
    )(raw, dead_mask, kernel, blob_wires)


def solution(mesh):
    return jax.shard_map(
        shards,
        mesh=mesh,
        in_specs=(P("apa", "band", "slab"), P("apa", "band"), P(), P(("apa", "band"), None)),
        out_specs=(P("apa", "band", "slab"), P(("apa", "band"), "slab")),
        check_vma=False,
    )
```

```python
import jax
import jax.numpy as jnp
from jax import lax
from jax.experimental import pallas as pl
from jax.experimental.pallas import tpu as pltpu
from jax.sharding import PartitionSpec as P

W = 2560
WR = 10
H = 128
TAPS = 2 * WR + 1
BANDS = 4
SLABS = 4
PLANES = 8
PEERS = 8
WIRES = W // BANDS
TICKS = 2 * H
LONG = 2 * TICKS
REACH = 3 * H
EDGE = 16
TALL = WIRES + 2 * EDGE
SLICES = TICKS // 2
SLOTS = 128
BLOBS = 768
PLACES = 12
COLS = 40
LANES = 128
GROUPS = 64
PICK_OWNERS = 8
CONV_GROUPS = tuple((u, u + 2) for u in range(0, 22, 2))
BF = jnp.bfloat16
F32 = jnp.float32
MESH = pl.DeviceIdType.MESH


def iota(shape, dim):
    return lax.broadcasted_iota(jnp.int32, shape, dim)


def dot(a, b):
    return jnp.dot(a, b, preferred_element_type=F32)


def build_tables(k_ref, k32, tab):
    k32[...] = jnp.zeros_like(k32)
    k32[0:TAPS, 0 : TICKS + 1] = k_ref[...].astype(F32)
    source = iota((H, H), 0)
    target = iota((H, H), 1)
    nothing = jnp.zeros((REACH, H), BF)
    tab[0, :, H:TICKS] = nothing
    tab[TAPS, :, 0:H] = nothing

    def one(p, carry):
        row = k32[pl.ds(p, 1), 0:TICKS]
        last = k32[pl.ds(p, 1), TICKS:LONG][:, 0:1]
        taps = pltpu.roll(jnp.broadcast_to(row, (TICKS, TICKS)), 0, 1, stride=1, stride_axis=0)
        near = taps[0:H, 0:H]
        first = jnp.where(source > target, near, jnp.where(target == source, last, 0.0)).astype(BF)
        second = taps[H:TICKS, 0:H].astype(BF)
        third = jnp.where(target >= source, near, 0.0).astype(BF)
        for n, part in enumerate((first, second, third)):
            tab[p, n * H : (n + 1) * H, 0:H] = part
            tab[p + 1, n * H : (n + 1) * H, H:TICKS] = part
        return carry

    lax.fori_loop(0, TAPS, one, 0)


def mask_waves(raw_ref, mask_ref, mask8, clean):
    mask8[...] = jnp.zeros_like(mask8)
    mask8[0:2, :] = mask_ref[...].astype(F32)
    live = jnp.transpose(mask8[...])
    for ap in range(2):
        wave = raw_ref[ap].astype(F32) * live[:, ap : ap + 1]
        clean[ap, EDGE : EDGE + WIRES, H : H + TICKS] = wave.astype(BF)


def interleave(clean, xf, xi, ap, has):
    left, right, above, below = has
    rows = ((0, EDGE, above), (EDGE, EDGE + WIRES, None), (EDGE + WIRES, TALL, below))
    cols = ((0, H, left), (H, H + TICKS, None), (H + TICKS, LONG, right))
    for r0, r1, row_ok in rows:
        for c0, c1, col_ok in cols:
            part = clean[ap, r0:r1, c0:c1].astype(F32)
            if row_ok is not None:
                part = jnp.where(row_ok, part, 0.0)
            if col_ok is not None:
                part = jnp.where(col_ok, part, 0.0)
            for t in range((c1 - c0) // LANES):
                xf[c0 // LANES + t, r0:r1, :] = part[:, t * LANES : (t + 1) * LANES]
    first = EDGE - WR

    def one(i, carry):
        for t in range(LONG // LANES):
            picked = xf[t, pl.ds(i + first, 16, stride=COLS), :]
            xi[ap, lax.div(i, 2), lax.rem(i, 2), :, t * LANES : (t + 1) * LANES] = picked.astype(BF)
        return carry

    lax.fori_loop(0, COLS + 2 * WR, one, 0, unroll=4)


def convolve(xi, tab, so, sig_v, held, pair_sum, ap):
    pairs = COLS // 2
    for tb in range(TICKS // H):
        total = None
        for u0, u1 in CONV_GROUPS:
            parts = [
                xi[ap, u // 2 : u // 2 + pairs, u % 2, :, tb * H : tb * H + REACH].reshape(
                    pairs * 16, REACH
                )
                for u in range(u0, u1)
            ]
            rhs = tab[u0:u1].reshape((u1 - u0) * REACH, TICKS)
            term = dot(jnp.concatenate(parts, axis=1), rhs)
            total = term if total is None else total + term
        for i in range(pairs):
            for n in range(2):
                so[tb, pl.ds(2 * i + n, 16, stride=COLS), :] = total[
                    16 * i : 16 * (i + 1), n * H : (n + 1) * H
                ]
    wave = jnp.concatenate([so[t] for t in range(TICKS // LANES)], axis=1).astype(BF)
    sig_v[ap] = wave
    held[0, ap * WIRES : (ap + 1) * WIRES, :] = dot(wave, pair_sum).astype(BF)


def tall(row, height):
    block = jnp.broadcast_to(row, (16, row.shape[1])).astype(BF)
    return jnp.concatenate([block] * (height // 16), axis=0)


def one_if(hit):
    return jnp.where(hit, jnp.ones((), BF), jnp.zeros((), BF))


def make_requests(wires_ref, request, bslot, hots, counts, upper):
    refs = wires_ref[...]
    usable = refs >= 0
    wire = jnp.where(usable, refs, 0)
    apa = ((wire >> 9) * 205) >> 10
    wire = wire - apa * W
    band = ((wire >> 7) * 205) >> 10
    row = (apa & 1) * WIRES + wire - band * WIRES
    source = jnp.where(usable, (apa >> 1) * BANDS + band, 255).astype(F32)
    row_high = ((row >> 7) + 1).astype(F32)
    row_low = (row & 127).astype(F32)
    blob = iota((1, BLOBS), 1)
    blob_high = tall(((blob >> 7) + 1).astype(F32), GROUPS)
    blob_low = tall((blob & 127).astype(F32), GROUPS)
    block = BLOBS // 3
    upper[0 : 2 * block, :] = jnp.ones((2 * block, block), BF)
    upper[2 * block :, :] = (
        (iota((block, block), 0) < iota((block, block), 1)).astype(F32).astype(BF)
    )
    group = iota((GROUPS, BLOBS), 0).astype(F32).astype(BF)
    slot = iota((SLOTS, BLOBS), 0).astype(F32).astype(BF)
    for k in range(PLACES):
        hots[k * GROUPS : (k + 1) * GROUPS, :] = one_if(group == tall(source[k : k + 1], GROUPS))
    for j in range(3):
        counts[:, j * block : (j + 1) * block] = dot(
            hots[:, 0 : (j + 1) * block], upper[(2 - j) * block :, :]
        )
    before = jnp.zeros((GROUPS, 1), F32)
    table = jnp.zeros((4 * GROUPS, SLOTS), F32)
    for k in range(PLACES):
        here = slice(k * GROUPS, (k + 1) * GROUPS)
        hot = hots[here, :]
        hot32 = hot.astype(F32)
        count = counts[here, :]
        rank = jnp.sum(hot32 * (count + before), axis=0, keepdims=True)
        before = before + (count + hot32)[:, BLOBS - 1 : BLOBS]
        slot_hot = one_if(slot == tall(rank, SLOTS))
        values = jnp.concatenate(
            [
                hot * tall(row_high[k : k + 1], GROUPS),
                hot * tall(row_low[k : k + 1], GROUPS),
                hot * blob_high,
                hot * blob_low,
            ],
            axis=0,
        )
        table = table + lax.dot_general(
            values, slot_hot, (((1,), (1,)), ((), ())), preferred_element_type=F32
        )
    request[...] = jnp.transpose(table[0 : 2 * GROUPS]).astype(BF)
    bslot[...] = table[2 * GROUPS :]


def pick(reqbox, held, picks, slot, plane, core, band):
    group = plane * 8 + core * BANDS + band
    index = iota((LANES, 2 * LANES), 0)
    choose = index == jnp.where(iota((LANES, 2 * LANES), 1) < LANES, group, group + GROUPS)
    choose = choose.astype(F32).astype(BF)
    height = PICK_OWNERS * SLOTS
    lane = iota((height, LANES), 1).astype(F32).astype(BF)

    def one(n, carry):
        at = pl.ds(PICK_OWNERS * n, PICK_OWNERS)
        asked = reqbox[at].reshape(height, LANES)
        wide = dot(asked, choose)
        high = wide[:, 0:LANES].astype(BF)
        low = one_if(wide[:, LANES:].astype(BF) == lane)
        tiles = [
            jnp.where(high == jnp.asarray(t + 1, BF), low, jnp.zeros((), BF))
            for t in range(2 * WIRES // LANES)
        ]
        got = dot(jnp.concatenate(tiles, axis=1), held[slot])
        picks[slot, at] = got.astype(BF).reshape(PICK_OWNERS, SLOTS, SLICES)
        return carry

    lax.fori_loop(0, PEERS // PICK_OWNERS, one, 0)


def place(bslot, picks, inbox, total, slot, plane, core, band):
    highs = []
    lows = []
    blocks = []
    blob = iota((SLOTS, LANES), 0).astype(F32).astype(BF)
    for r in range(PEERS):
        dc, dy = divmod(r, BANDS)
        from_core = lax.rem(core + dc, 2)
        from_band = lax.rem(band + BANDS - dy, BANDS)
        group = plane * 8 + from_core * BANDS + from_band
        highs.append(tall(bslot[pl.ds(group, 1), :], SLOTS))
        lows.append(one_if(blob == tall(bslot[pl.ds(group + GROUPS, 1), :], SLOTS)))
        blocks.append(picks[slot, 0] if r == 0 else inbox[slot, r])
    incoming = jnp.concatenate(blocks, axis=0)
    high = jnp.concatenate(highs, axis=1)
    low = jnp.concatenate(lows, axis=1)
    hot = jnp.concatenate(
        [
            jnp.where(high == jnp.asarray(m + 1, BF), low, jnp.zeros((), BF))
            for m in range(BLOBS // LANES)
        ],
        axis=0,
    )
    total[...] = total[...] + dot(hot, incoming)


def whole(
    raw_ref, mask_ref, k_ref, wires_ref, sig_ref, blob_ref,
    clean, xf, xi, tab, k32, mask8, so, sig_v, held, hots, counts, upper, request, bslot,
    reqbox, picks, inbox,
    halo_send, halo_recv, req_send, req_recv, ring_send, ring_recv, box_send, box_recv, out_sem,
):
    apa = lax.axis_index("apa")
    slab = lax.axis_index("slab")
    band = lax.axis_index("band")
    plane = lax.div(apa, 2)
    core = lax.rem(apa, 2)

    def device(dz=0, dc=0, dx=0, dy=0):
        z = lax.rem(plane + dz + PLANES, PLANES)
        c = lax.rem(core + dc, 2)
        return (z * 2 + c, lax.rem(slab + dx + SLABS, SLABS), lax.rem(band + dy + BANDS, BANDS))

    peers = [device(dc=r // BANDS, dy=r % BANDS) for r in range(PEERS)]
    everyone = peers[1:] + [device(dz=1), device(dz=-1), device(dx=1), device(dx=-1)]
    everyone += [device(dx=i, dy=j) for i in (-1, 1) for j in (-1, 1)]
    barrier = pltpu.get_barrier_semaphore()
    for other in everyone:
        pl.semaphore_signal(barrier, inc=1, device_id=other, device_id_type=MESH)

    mask_waves(raw_ref, mask_ref, mask8, clean)
    pl.semaphore_wait(barrier, len(everyone))

    def remote(src, dst, send, recv, to):
        return pltpu.make_async_remote_copy(
            src_ref=src, dst_ref=dst, send_sem=send, recv_sem=recv, device_id=to, device_id_type=MESH
        )

    own = slice(EDGE, EDGE + WIRES)
    mid = slice(H, H + TICKS)
    row_parts = {
        -1: (slice(EDGE, 2 * EDGE), slice(EDGE + WIRES, TALL)),
        0: (own, own),
        1: (slice(WIRES, EDGE + WIRES), slice(0, EDGE)),
    }
    col_parts = {
        -1: (slice(H, 2 * H), slice(H + TICKS, LONG)),
        0: (mid, mid),
        1: (slice(2 * H, 3 * H), slice(0, H)),
    }
    halos = {0: [], 1: []}
    number = 0
    for ap in range(2):
        for dx in (-1, 0, 1):
            for dy in (-1, 0, 1):
                if dx == 0 and dy == 0:
                    continue
                (rs, rd), (cs, cd) = row_parts[dy], col_parts[dx]
                copy = remote(
                    clean.at[ap, rs, cs], clean.at[ap, rd, cd],
                    halo_send.at[number], halo_recv.at[number], device(dx=dx, dy=dy),
                )
                copy.start()
                halos[ap].append(copy)
                number += 1

    make_requests(wires_ref, request, bslot, hots, counts, upper)
    reqbox[0] = request[...]
    asks = []
    for r in range(1, PEERS):
        dc, dy = divmod(r, BANDS)
        back = dc * BANDS + (BANDS - dy) % BANDS
        copy = remote(request, reqbox.at[back], req_send.at[back], req_recv.at[back], peers[r])
        copy.start()
        asks.append(copy)

    build_tables(k_ref, k32, tab)
    pair_sum = (iota((TICKS, SLICES), 0) >> 1) == iota((TICKS, SLICES), 1)
    pair_sum = pair_sum.astype(F32).astype(BF)
    has = (slab > 0, slab < SLABS - 1, band > 0, band < BANDS - 1)

    def half(ap):
        return slice(ap * WIRES, (ap + 1) * WIRES)

    towards = (device(dz=1), device(dz=-1))

    def slot_at(way, distance):
        if distance == 0:
            return 0
        if distance == 4:
            return 7
        return distance + 3 * way

    def ring(way, distance, ap):
        number = 2 * (distance - 1) + (ap if distance < 4 else 0)
        return remote(
            held.at[slot_at(way, distance - 1), half(ap)],
            held.at[slot_at(way, distance), half(ap)],
            ring_send.at[way, number], ring_recv.at[way, number], towards[way],
        )

    writes = []
    started = []
    for ap in range(2):
        for copy in halos[ap]:
            copy.wait_recv()
        interleave(clean, xf, xi, ap, has)
        convolve(xi, tab, so, sig_v, held, pair_sum, ap)
        for way in range(2):
            copy = ring(way, 1, ap)
            copy.start()
            started.append(copy)
        write = pltpu.make_async_copy(sig_v.at[ap], sig_ref.at[ap], out_sem.at[ap])
        write.start()
        writes.append(write)

    blob_ref[...] = jnp.zeros_like(blob_ref)
    for copy in asks:
        copy.wait_recv()
    boxes = {}

    def serve(slot, shift):
        source = lax.rem(plane + shift + PLANES, PLANES)
        pick(reqbox, held, picks, slot, source, core, band)
        boxes[slot] = []
        for r in range(1, PEERS):
            copy = remote(
                picks.at[slot, r], inbox.at[slot, r], box_send.at[slot, r], box_recv.at[slot, r], peers[r]
            )
            copy.start()
            boxes[slot].append(copy)

    def collect(slot, shift):
        source = lax.rem(plane + shift + PLANES, PLANES)
        for copy in boxes[slot]:
            copy.wait_recv()
        place(bslot, picks, inbox, blob_ref, slot, source, core, band)

    def forward(distance, ap):
        for way in range(2):
            ring(way, distance, ap).wait_recv()
            if distance < 3 or ap == way:
                copy = ring(way, distance + 1, ap)
                copy.start()
                started.append(copy)

    serve(0, 0)
    forward(1, 0)
    collect(0, 0)
    forward(1, 1)
    serve(1, -1)
    forward(2, 0)
    serve(4, 1)
    collect(1, -1)
    forward(2, 1)
    serve(2, -2)
    collect(4, 1)
    forward(3, 0)
    serve(5, 2)
    collect(2, -2)
    forward(3, 1)
    serve(3, -3)
    serve(6, 3)
    collect(5, 2)
    collect(3, -3)
    ring(0, 4, 0).wait_recv()
    ring(1, 4, 1).wait_recv()
    serve(7, 4)
    collect(6, 3)
    collect(7, 4)

    for copies in (halos[0], halos[1], asks, started, *boxes.values()):
        for copy in copies:
            copy.wait_send()
    for write in writes:
        write.wait()


def shards(raw, dead_mask, kernel, blob_wires):
    vmem = pl.BlockSpec(memory_space=pltpu.VMEM)
    dma = pltpu.SemaphoreType.DMA
    return pl.pallas_call(
        whole,
        out_shape=(
            jax.ShapeDtypeStruct((2, WIRES, TICKS), BF),
            jax.ShapeDtypeStruct((BLOBS, SLICES), F32),
        ),
        in_specs=[vmem] * 4,
        out_specs=(pl.BlockSpec(memory_space=pl.ANY), vmem),
        scratch_shapes=[
            pltpu.VMEM((2, TALL, LONG), BF),
            pltpu.VMEM((LONG // LANES, TALL, LANES), F32),
            pltpu.VMEM((2, COLS // 2 + WR, 2, 16, LONG), BF),
            pltpu.VMEM((TAPS + 1, REACH, TICKS), BF),
            pltpu.VMEM((24, LONG), F32),
            pltpu.VMEM((8, WIRES), F32),
            pltpu.VMEM((TICKS // LANES, WIRES, LANES), F32),
            pltpu.VMEM((2, WIRES, TICKS), BF),
            pltpu.VMEM((PLANES, 2 * WIRES, SLICES), BF),
            pltpu.VMEM((PLACES * GROUPS, BLOBS), BF),
            pltpu.VMEM((PLACES * GROUPS, BLOBS), F32),
            pltpu.VMEM((BLOBS, BLOBS // 3), BF),
            pltpu.VMEM((SLOTS, LANES), BF),
            pltpu.VMEM((LANES, SLOTS), F32),
            pltpu.VMEM((PEERS, SLOTS, LANES), BF),
            pltpu.VMEM((PLANES, PEERS, SLOTS, SLICES), BF),
            pltpu.VMEM((PLANES, PEERS, SLOTS, SLICES), BF),
            dma((16,)),
            dma((16,)),
            dma((PEERS,)),
            dma((PEERS,)),
            dma((2, 7)),
            dma((2, 7)),
            dma((PLANES, PEERS)),
            dma((PLANES, PEERS)),
            dma((2,)),
        ],
        compiler_params=pltpu.CompilerParams(
            collective_id=0, has_side_effects=True, vmem_limit_bytes=56 << 20
        ),
    )(raw, dead_mask, kernel, blob_wires.T)


def solution(mesh):
    return jax.shard_map(
        shards,
        mesh=mesh,
        in_specs=(P("apa", "band", "slab"), P("apa", "band"), P(), P(("apa", "band"), None)),
        out_specs=(P("apa", "band", "slab"), P(("apa", "band"), "slab")),
        check_vma=False,
    )
```

```python
import jax
import jax.numpy as jnp
from jax import lax
from jax.experimental import pallas as pl
from jax.experimental.pallas import tpu as pltpu
from jax.sharding import PartitionSpec as P

W = 2560
WR = 10
H = 128
TAPS = 2 * WR + 1
BANDS = 4
SLABS = 4
PLANES = 8
PEERS = 8
WIRES = W // BANDS
TICKS = 2 * H
LONG = 2 * TICKS
REACH = 3 * H
EDGE = 16
TALL = WIRES + 2 * EDGE
SLICES = TICKS // 2
SLOTS = 128
BLOBS = 768
PLACES = 12
COLS = 40
LANES = 128
GROUPS = 64
PICK_OWNERS = 8
PARTS = 2
CONV_GROUPS = tuple((u, u + 2) for u in range(0, 22, 2))
BF = jnp.bfloat16
F32 = jnp.float32
MESH = pl.DeviceIdType.MESH


def iota(shape, dim):
    return lax.broadcasted_iota(jnp.int32, shape, dim)


def dot(a, b):
    return jnp.dot(a, b, preferred_element_type=F32)


def build_tables(k_ref, k32, tab):
    k32[...] = jnp.zeros_like(k32)
    k32[0:TAPS, 0 : TICKS + 1] = k_ref[...].astype(F32)
    source = iota((H, H), 0)
    target = iota((H, H), 1)
    nothing = jnp.zeros((REACH, H), BF)
    tab[0, :, H:TICKS] = nothing
    tab[TAPS, :, 0:H] = nothing

    def one(p, carry):
        row = k32[pl.ds(p, 1), 0:TICKS]

        def turned(start):
            piece = jnp.broadcast_to(row[:, start : start + H], (H, H))
            return pltpu.roll(piece, 0, 1, stride=1, stride_axis=0)

        last = k32[pl.ds(p, 1), TICKS:LONG][:, 0:1]
        early, late = turned(0), turned(H)
        first = jnp.where(source > target, late, jnp.where(target == source, last, 0.0)).astype(BF)
        second = jnp.where(target >= source, late, early).astype(BF)
        third = jnp.where(target >= source, early, 0.0).astype(BF)
        for n, part in enumerate((first, second, third)):
            tab[p, n * H : (n + 1) * H, 0:H] = part
            tab[p + 1, n * H : (n + 1) * H, H:TICKS] = part
        return carry

    lax.fori_loop(0, TAPS, one, 0, unroll=3)


def mask_waves(raw_ref, mask8, clean):
    live = jnp.transpose(mask8[...])
    for ap in range(2):
        wave = raw_ref[ap].astype(F32) * live[:, ap : ap + 1]
        clean[ap, EDGE : EDGE + WIRES, H : H + TICKS] = wave.astype(BF)


def interleave(clean, xf, xi, ap, has):
    left, right, above, below = has
    rows = ((0, EDGE, above), (EDGE, EDGE + WIRES, None), (EDGE + WIRES, TALL, below))
    cols = ((0, H, left), (H, H + TICKS, None), (H + TICKS, LONG, right))
    for r0, r1, row_ok in rows:
        for c0, c1, col_ok in cols:
            part = clean[ap, r0:r1, c0:c1].astype(F32)
            if row_ok is not None:
                part = jnp.where(row_ok, part, 0.0)
            if col_ok is not None:
                part = jnp.where(col_ok, part, 0.0)
            for t in range((c1 - c0) // LANES):
                xf[c0 // LANES + t, r0:r1, :] = part[:, t * LANES : (t + 1) * LANES]
    first = EDGE - WR

    def one(i, carry):
        for t in range(LONG // LANES):
            picked = xf[t, pl.ds(i + first, 16, stride=COLS), :]
            picked = picked.astype(BF)
            if t < 3:
                xi[ap, lax.div(i, 2), lax.rem(i, 2), 0, :, t * LANES : (t + 1) * LANES] = picked
            if t > 0:
                xi[ap, lax.div(i, 2), lax.rem(i, 2), 1, :, (t - 1) * LANES : t * LANES] = picked
        return carry

    lax.fori_loop(0, COLS + 2 * WR, one, 0, unroll=4)


def convolve(xi, tab, so, waves, held, pair_sum, ap, part):
    pairs = COLS // (2 * PARTS)
    first = part * pairs
    total = None
    for u0, u1 in CONV_GROUPS:
        pieces = [
            xi[ap, first + u // 2 : first + u // 2 + pairs, u % 2].reshape(pairs * 32, REACH)
            for u in range(u0, u1)
        ]
        rhs = tab[u0:u1].reshape((u1 - u0) * REACH, TICKS)
        term = dot(jnp.concatenate(pieces, axis=1), rhs)
        total = term if total is None else total + term
    rows = pairs * 16
    total = total.reshape(pairs, 2, 16, TICKS)
    for n in range(2):
        ends = [total[:, tb, :, n * H : (n + 1) * H].reshape(rows, H) for tb in range(2)]
        for tb, end in enumerate(ends):
            waves[n * rows : (n + 1) * rows, tb * H : (tb + 1) * H] = end.astype(BF)
            for i in range(pairs):
                wire = 2 * (first + i) + n
                so[tb, pl.ds(wire, 16, stride=COLS), :] = end[16 * i : 16 * (i + 1)]
    start = (ap * PARTS + part) * 2 * rows

    def pairwise(n, carry):
        at = pl.ds(pl.multiple_of(n * rows, rows), rows)
        to = pl.ds(pl.multiple_of(start + n * rows, rows), rows)
        held[0, to, :] = dot(waves[at, :], pair_sum[...]).astype(BF)
        return carry

    lax.fori_loop(0, 2, pairwise, 0)


def tall(row, height):
    block = jnp.broadcast_to(row, (16, row.shape[1])).astype(BF)
    return jnp.concatenate([block] * (height // 16), axis=0)


def one_if(hit):
    return jnp.where(hit, jnp.ones((), BF), jnp.zeros((), BF))


def make_requests(wires_ref, request, bslot, hots, counts, upper):
    refs = wires_ref[...]
    usable = refs >= 0
    wire = jnp.where(usable, refs, 0)
    apa = ((wire >> 9) * 205) >> 10
    wire = wire - apa * W
    band = ((wire >> 7) * 205) >> 10
    wire = wire - band * WIRES
    column = (wire * 1639) >> 16
    wire = wire - column * COLS
    pair = wire >> 1
    part = jnp.where(pair >= COLS // 4, 1, 0)
    row = (apa & 1) * WIRES + part * (WIRES // 2) + (wire & 1) * (WIRES // 4)
    row = row + (pair - part * (COLS // 4)) * 16 + column
    source = jnp.where(usable, (apa >> 1) * BANDS + band, 255).astype(F32)
    row_high = ((row >> 7) + 1).astype(F32)
    row_low = (row & 127).astype(F32)
    blob = iota((1, BLOBS), 1)
    blob_high = tall(((blob >> 7) + 1).astype(F32), GROUPS)
    blob_low = tall((blob & 127).astype(F32), GROUPS)
    block = BLOBS // 3
    upper[0 : 2 * block, :] = jnp.ones((2 * block, block), BF)
    upper[2 * block :, :] = (
        (iota((block, block), 0) < iota((block, block), 1)).astype(F32).astype(BF)
    )
    group = iota((GROUPS, BLOBS), 0).astype(F32).astype(BF)
    slot = iota((SLOTS, BLOBS), 0).astype(F32).astype(BF)
    for k in range(PLACES):
        hots[k * GROUPS : (k + 1) * GROUPS, :] = one_if(group == tall(source[k : k + 1], GROUPS))
    for j in range(3):
        counts[:, j * block : (j + 1) * block] = dot(
            hots[:, 0 : (j + 1) * block], upper[(2 - j) * block :, :]
        )
    before = jnp.zeros((GROUPS, 1), F32)
    table = jnp.zeros((4 * GROUPS, SLOTS), F32)
    for k in range(PLACES):
        here = slice(k * GROUPS, (k + 1) * GROUPS)
        hot = hots[here, :]
        hot32 = hot.astype(F32)
        count = counts[here, :]
        rank = jnp.sum(hot32 * (count + before), axis=0, keepdims=True)
        before = before + (count + hot32)[:, BLOBS - 1 : BLOBS]
        slot_hot = one_if(slot == tall(rank, SLOTS))
        values = jnp.concatenate(
            [
                hot * tall(row_high[k : k + 1], GROUPS),
                hot * tall(row_low[k : k + 1], GROUPS),
                hot * blob_high,
                hot * blob_low,
            ],
            axis=0,
        )
        table = table + lax.dot_general(
            values, slot_hot, (((1,), (1,)), ((), ())), preferred_element_type=F32
        )
    request[...] = jnp.transpose(table[0 : 2 * GROUPS]).astype(BF)
    bslot[...] = table[2 * GROUPS :]


def pick(reqbox, held, picks, slot, plane, core, band):
    group = plane * 8 + core * BANDS + band
    index = iota((LANES, 2 * LANES), 0)
    choose = index == jnp.where(iota((LANES, 2 * LANES), 1) < LANES, group, group + GROUPS)
    choose = choose.astype(F32).astype(BF)
    height = PICK_OWNERS * SLOTS
    lane = iota((height, LANES), 1).astype(F32).astype(BF)

    def one(n, carry):
        at = pl.ds(PICK_OWNERS * n, PICK_OWNERS)
        asked = reqbox[at].reshape(height, LANES)
        wide = dot(asked, choose)
        high = wide[:, 0:LANES].astype(BF)
        low = one_if(wide[:, LANES:].astype(BF) == lane)
        tiles = [
            jnp.where(high == jnp.asarray(t + 1, BF), low, jnp.zeros((), BF))
            for t in range(2 * WIRES // LANES)
        ]
        got = dot(jnp.concatenate(tiles, axis=1), held[slot])
        picks[slot, at] = got.astype(BF).reshape(PICK_OWNERS, SLOTS, SLICES)
        return carry

    lax.fori_loop(0, PEERS // PICK_OWNERS, one, 0)


def place(bslot, picks, inbox, total, slot, plane, core, band):
    highs = []
    lows = []
    blocks = []
    blob = iota((SLOTS, LANES), 0).astype(F32).astype(BF)
    for r in range(PEERS):
        dc, dy = divmod(r, BANDS)
        from_core = lax.rem(core + dc, 2)
        from_band = lax.rem(band + BANDS - dy, BANDS)
        group = plane * 8 + from_core * BANDS + from_band
        highs.append(tall(bslot[pl.ds(group, 1), :], SLOTS))
        lows.append(one_if(blob == tall(bslot[pl.ds(group + GROUPS, 1), :], SLOTS)))
        blocks.append(picks[slot, 0] if r == 0 else inbox[slot, r])
    incoming = jnp.concatenate(blocks, axis=0)
    high = jnp.concatenate(highs, axis=1)
    low = jnp.concatenate(lows, axis=1)
    hot = jnp.concatenate(
        [
            jnp.where(high == jnp.asarray(m + 1, BF), low, jnp.zeros((), BF))
            for m in range(BLOBS // LANES)
        ],
        axis=0,
    )
    total[...] = total[...] + dot(hot, incoming)


def whole(
    raw_ref, mask_ref, k_ref, wires_ref, sig_ref, blob_ref,
    clean, xf, xi, tab, k32, mask8, so, waves, pair_sum, sig_v, held, hots, counts, upper, request, bslot,
    reqbox, picks, inbox,
    halo_send, halo_recv, req_send, req_recv, ring_send, ring_recv, box_send, box_recv, out_sem,
):
    fetch = pltpu.make_async_copy(raw_ref, sig_v, out_sem.at[2])
    fetch.start()
    apa = lax.axis_index("apa")
    slab = lax.axis_index("slab")
    band = lax.axis_index("band")
    plane = lax.div(apa, 2)
    core = lax.rem(apa, 2)

    def device(dz=0, dc=0, dx=0, dy=0):
        z = lax.rem(plane + dz + PLANES, PLANES)
        c = lax.rem(core + dc, 2)
        return (z * 2 + c, lax.rem(slab + dx + SLABS, SLABS), lax.rem(band + dy + BANDS, BANDS))

    peers = [device(dc=r // BANDS, dy=r % BANDS) for r in range(PEERS)]
    everyone = peers[1:] + [device(dz=1), device(dz=-1), device(dx=1), device(dx=-1)]
    everyone += [device(dx=i, dy=j) for i in (-1, 1) for j in (-1, 1)]
    barrier = pltpu.get_barrier_semaphore()
    for other in everyone:
        pl.semaphore_signal(barrier, inc=1, device_id=other, device_id_type=MESH)

    mask8[...] = jnp.zeros_like(mask8)
    mask8[0:2, :] = mask_ref[...].astype(F32)
    fetch.wait()
    mask_waves(sig_v, mask8, clean)
    pl.semaphore_wait(barrier, len(everyone))

    def remote(src, dst, send, recv, to):
        return pltpu.make_async_remote_copy(
            src_ref=src, dst_ref=dst, send_sem=send, recv_sem=recv, device_id=to, device_id_type=MESH
        )

    own = slice(EDGE, EDGE + WIRES)
    mid = slice(H, H + TICKS)
    row_parts = {
        -1: (slice(EDGE, 2 * EDGE), slice(EDGE + WIRES, TALL)),
        0: (own, own),
        1: (slice(WIRES, EDGE + WIRES), slice(0, EDGE)),
    }
    col_parts = {
        -1: (slice(H, 2 * H), slice(H + TICKS, LONG)),
        0: (mid, mid),
        1: (slice(2 * H, 3 * H), slice(0, H)),
    }
    halos = {0: [], 1: []}
    number = 0
    for ap in range(2):
        for dx in (-1, 0, 1):
            for dy in (-1, 0, 1):
                if dx == 0 and dy == 0:
                    continue
                (rs, rd), (cs, cd) = row_parts[dy], col_parts[dx]
                copy = remote(
                    clean.at[ap, rs, cs], clean.at[ap, rd, cd],
                    halo_send.at[number], halo_recv.at[number], device(dx=dx, dy=dy),
                )
                copy.start()
                halos[ap].append(copy)
                number += 1

    build_tables(k_ref, k32, tab)
    pair_hit = (iota((TICKS, SLICES), 0) >> 1) == iota((TICKS, SLICES), 1)
    pair_sum[...] = pair_hit.astype(F32).astype(BF)
    make_requests(wires_ref, request, bslot, hots, counts, upper)
    reqbox[0] = request[...]
    asks = []
    for r in range(1, PEERS):
        dc, dy = divmod(r, BANDS)
        back = dc * BANDS + (BANDS - dy) % BANDS
        copy = remote(request, reqbox.at[back], req_send.at[back], req_recv.at[back], peers[r])
        copy.start()
        asks.append(copy)

    has = (slab > 0, slab < SLABS - 1, band > 0, band < BANDS - 1)

    towards = (device(dz=1), device(dz=-1))
    quarter = WIRES // PARTS

    def slot_at(way, distance):
        if distance == 0:
            return 0
        if distance == 4:
            return 7
        return distance + 3 * way

    def ring(way, distance, piece):
        if distance == 1:
            number, rows = piece, slice(piece * quarter, (piece + 1) * quarter)
        else:
            number = 4 + 2 * (distance - 2) + (piece if distance < 4 else 0)
            rows = slice(piece * WIRES, (piece + 1) * WIRES)
        return remote(
            held.at[slot_at(way, distance - 1), rows],
            held.at[slot_at(way, distance), rows],
            ring_send.at[way, number], ring_recv.at[way, number], towards[way],
        )

    writes = []
    started = []
    for ap in range(2):
        for copy in halos[ap]:
            copy.wait_recv()
        interleave(clean, xf, xi, ap, has)
        for part in range(PARTS):
            convolve(xi, tab, so.at[ap], waves, held, pair_sum, ap, part)
            for way in range(2):
                copy = ring(way, 1, ap * PARTS + part)
                copy.start()
                started.append(copy)

    def write_signal(ap):
        sig_v[ap] = jnp.concatenate([so[ap, t] for t in range(TICKS // LANES)], axis=1).astype(BF)
        write = pltpu.make_async_copy(sig_v.at[ap], sig_ref.at[ap], out_sem.at[ap])
        write.start()
        writes.append(write)

    boxes = {}

    def serve(slot, shift):
        source = lax.rem(plane + shift + PLANES, PLANES)
        pick(reqbox, held, picks, slot, source, core, band)
        boxes[slot] = []
        for r in range(1, PEERS):
            copy = remote(
                picks.at[slot, r], inbox.at[slot, r], box_send.at[slot, r], box_recv.at[slot, r], peers[r]
            )
            copy.start()
            boxes[slot].append(copy)

    def collect(slot, shift):
        source = lax.rem(plane + shift + PLANES, PLANES)
        for copy in boxes[slot]:
            copy.wait_recv()
        place(bslot, picks, inbox, blob_ref, slot, source, core, band)

    def forward(distance, half):
        for way in range(2):
            if distance == 1:
                for part in range(PARTS):
                    ring(way, 1, half * PARTS + part).wait_recv()
            else:
                ring(way, distance, half).wait_recv()
            if distance < 3 or half == way:
                copy = ring(way, distance + 1, half)
                copy.start()
                started.append(copy)

    forward(1, 0)
    for copy in asks:
        copy.wait_recv()
    serve(0, 0)
    write_signal(0)
    forward(1, 1)
    serve(1, -1)
    serve(4, 1)
    write_signal(1)
    blob_ref[...] = jnp.zeros_like(blob_ref)
    forward(2, 0)
    collect(0, 0)
    forward(2, 1)
    serve(2, -2)
    serve(5, 2)
    collect(1, -1)
    collect(4, 1)
    forward(3, 0)
    forward(3, 1)
    serve(3, -3)
    serve(6, 3)
    collect(2, -2)
    collect(5, 2)
    ring(0, 4, 0).wait_recv()
    ring(1, 4, 1).wait_recv()
    serve(7, 4)
    collect(3, -3)
    collect(6, 3)
    collect(7, 4)

    for copies in (halos[0], halos[1], asks, started, *boxes.values()):
        for copy in copies:
            copy.wait_send()
    for write in writes:
        write.wait()


def hand_over(signal, charge):
    def body(signal_in, charge_in, signal_out, charge_out):
        signal_out[...] = signal_in[...]
        charge_out[...] = charge_in[...]

    steps = 2
    wave = pl.BlockSpec((2 // steps, WIRES, TICKS), lambda i: (i, 0, 0))
    blob = pl.BlockSpec((BLOBS // steps, SLICES), lambda i: (i, 0))
    return pl.pallas_call(
        body,
        grid=(steps,),
        out_shape=tuple(jax.ShapeDtypeStruct(x.shape, x.dtype) for x in (signal, charge)),
        in_specs=[wave, blob],
        out_specs=(wave, blob),
    )(signal, charge)


def shards(raw, dead_mask, kernel, blob_wires):
    vmem = pl.BlockSpec(memory_space=pltpu.VMEM)
    dma = pltpu.SemaphoreType.DMA
    signal, charge = pl.pallas_call(
        whole,
        out_shape=(
            jax.ShapeDtypeStruct((2, WIRES, TICKS), BF),
            jax.ShapeDtypeStruct((BLOBS, SLICES), F32),
        ),
        in_specs=[pl.BlockSpec(memory_space=pl.ANY)] + [vmem] * 3,
        out_specs=(pl.BlockSpec(memory_space=pl.ANY), vmem),
        scratch_shapes=[
            pltpu.VMEM((2, TALL, LONG), BF),
            pltpu.VMEM((LONG // LANES, TALL, LANES), F32),
            pltpu.VMEM((2, COLS // 2 + WR, 2, 2, 16, REACH), BF),
            pltpu.VMEM((TAPS + 1, REACH, TICKS), BF),
            pltpu.VMEM((24, LONG), F32),
            pltpu.VMEM((8, WIRES), F32),
            pltpu.VMEM((2, TICKS // LANES, WIRES, LANES), F32),
            pltpu.VMEM((WIRES // PARTS, TICKS), BF),
            pltpu.VMEM((TICKS, SLICES), BF),
            pltpu.VMEM((2, WIRES, TICKS), BF),
            pltpu.VMEM((PLANES, 2 * WIRES, SLICES), BF),
            pltpu.VMEM((PLACES * GROUPS, BLOBS), BF),
            pltpu.VMEM((PLACES * GROUPS, BLOBS), F32),
            pltpu.VMEM((BLOBS, BLOBS // 3), BF),
            pltpu.VMEM((SLOTS, LANES), BF),
            pltpu.VMEM((LANES, SLOTS), F32),
            pltpu.VMEM((PEERS, SLOTS, LANES), BF),
            pltpu.VMEM((PLANES, PEERS, SLOTS, SLICES), BF),
            pltpu.VMEM((PLANES, PEERS, SLOTS, SLICES), BF),
            dma((16,)),
            dma((16,)),
            dma((PEERS,)),
            dma((PEERS,)),
            dma((2, 9)),
            dma((2, 9)),
            dma((PLANES, PEERS)),
            dma((PLANES, PEERS)),
            dma((3,)),
        ],
        compiler_params=pltpu.CompilerParams(
            collective_id=0, has_side_effects=True, vmem_limit_bytes=56 << 20
        ),
    )(raw, dead_mask, kernel, blob_wires.T)
    return hand_over(signal, charge)


def solution(mesh):
    return jax.shard_map(
        shards,
        mesh=mesh,
        in_specs=(P("apa", "band", "slab"), P("apa", "band"), P(), P(("apa", "band"), None)),
        out_specs=(P("apa", "band", "slab"), P(("apa", "band"), "slab")),
        check_vma=False,
    )
```

```python
import jax
import jax.numpy as jnp
from jax import lax
from jax.experimental import pallas as pl
from jax.experimental.pallas import tpu as pltpu
from jax.sharding import PartitionSpec as P

W = 2560
WR = 10
H = 128
TAPS = 2 * WR + 1
BANDS = 4
SLABS = 4
PLANES = 8
PEERS = 8
WIRES = W // BANDS
TICKS = 2 * H
LONG = 2 * TICKS
REACH = 3 * H
EDGE = 16
TALL = WIRES + 2 * EDGE
SLICES = TICKS // 2
SLOTS = 128
BLOBS = 768
PLACES = 12
COLS = 40
LANES = 128
GROUPS = 64
PICK_OWNERS = 8
PARTS = 2
CONV_GROUPS = tuple((u, u + 2) for u in range(0, 22, 2))
BF = jnp.bfloat16
F32 = jnp.float32
MESH = pl.DeviceIdType.MESH


def iota(shape, dim):
    return lax.broadcasted_iota(jnp.int32, shape, dim)


def dot(a, b):
    return jnp.dot(a, b, preferred_element_type=F32)


def build_tables(k_ref, k32, tab):
    k32[...] = jnp.zeros_like(k32)
    k32[0:TAPS, 0 : TICKS + 1] = k_ref[...].astype(F32)
    source = iota((H, H), 0)
    target = iota((H, H), 1)
    nothing = jnp.zeros((REACH, H), BF)
    tab[0, :, H:TICKS] = nothing
    tab[TAPS, :, 0:H] = nothing

    def one(p, carry):
        row = k32[pl.ds(p, 1), 0:TICKS]

        def turned(start):
            piece = jnp.broadcast_to(row[:, start : start + H], (H, H))
            return pltpu.roll(piece, 0, 1, stride=1, stride_axis=0)

        last = k32[pl.ds(p, 1), TICKS:LONG][:, 0:1]
        early, late = turned(0), turned(H)
        first = jnp.where(source > target, late, jnp.where(target == source, last, 0.0)).astype(BF)
        second = jnp.where(target >= source, late, early).astype(BF)
        third = jnp.where(target >= source, early, 0.0).astype(BF)
        for n, part in enumerate((first, second, third)):
            tab[p, n * H : (n + 1) * H, 0:H] = part
            tab[p + 1, n * H : (n + 1) * H, H:TICKS] = part
        return carry

    lax.fori_loop(0, TAPS, one, 0, unroll=TAPS)


def mask_waves(raw, live, clean, ap):
    wave = raw[ap].astype(F32) * live[:, ap : ap + 1]
    clean[ap, EDGE : EDGE + WIRES, H : H + TICKS] = wave.astype(BF)


def interleave(clean, xf, xi, ap, has):
    left, right, above, below = has
    rows = ((0, EDGE, above), (EDGE, EDGE + WIRES, None), (EDGE + WIRES, TALL, below))
    cols = ((0, H, left), (H, H + TICKS, None), (H + TICKS, LONG, right))
    for r0, r1, row_ok in rows:
        for c0, c1, col_ok in cols:
            part = clean[ap, r0:r1, c0:c1].astype(F32)
            if row_ok is not None:
                part = jnp.where(row_ok, part, 0.0)
            if col_ok is not None:
                part = jnp.where(col_ok, part, 0.0)
            for t in range((c1 - c0) // LANES):
                xf[c0 // LANES + t, r0:r1, :] = part[:, t * LANES : (t + 1) * LANES]
    first = EDGE - WR

    def one(i, carry):
        for t in range(LONG // LANES):
            picked = xf[t, pl.ds(i + first, 16, stride=COLS), :]
            picked = picked.astype(BF)
            if t < 3:
                xi[ap, lax.div(i, 2), lax.rem(i, 2), 0, :, t * LANES : (t + 1) * LANES] = picked
            if t > 0:
                xi[ap, lax.div(i, 2), lax.rem(i, 2), 1, :, (t - 1) * LANES : t * LANES] = picked
        return carry

    lax.fori_loop(0, COLS + 2 * WR, one, 0, unroll=COLS + 2 * WR)


def convolve(xi, tab, so, waves, held, pair_sum, ap, part):
    pairs = COLS // (2 * PARTS)
    first = part * pairs
    total = None
    for u0, u1 in CONV_GROUPS:
        pieces = [
            xi[ap, first + u // 2 : first + u // 2 + pairs, u % 2].reshape(pairs * 32, REACH)
            for u in range(u0, u1)
        ]
        rhs = tab[u0:u1].reshape((u1 - u0) * REACH, TICKS)
        term = dot(jnp.concatenate(pieces, axis=1), rhs)
        total = term if total is None else total + term
    rows = pairs * 16
    total = total.reshape(pairs, 2, 16, TICKS)
    for n in range(2):
        ends = [total[:, tb, :, n * H : (n + 1) * H].reshape(rows, H) for tb in range(2)]
        for tb, end in enumerate(ends):
            waves[n * rows : (n + 1) * rows, tb * H : (tb + 1) * H] = end.astype(BF)
            for i in range(pairs):
                wire = 2 * (first + i) + n
                so[tb, pl.ds(wire, 16, stride=COLS), :] = end[16 * i : 16 * (i + 1)]
    start = (ap * PARTS + part) * 2 * rows

    def pairwise(n, carry):
        at = pl.ds(pl.multiple_of(n * rows, rows), rows)
        to = pl.ds(pl.multiple_of(start + n * rows, rows), rows)
        held[0, to, :] = dot(waves[at, :], pair_sum[...]).astype(BF)
        return carry

    lax.fori_loop(0, 2, pairwise, 0)


def tall(row, height):
    block = jnp.broadcast_to(row, (16, row.shape[1])).astype(BF)
    return jnp.concatenate([block] * (height // 16), axis=0)


def one_if(hit):
    return jnp.where(hit, jnp.ones((), BF), jnp.zeros((), BF))


def count_places(wires_ref, fields, hots, counts, upper):
    refs = wires_ref[...]
    usable = refs >= 0
    wire = jnp.where(usable, refs, 0)
    apa = ((wire >> 9) * 205) >> 10
    wire = wire - apa * W
    band = ((wire >> 7) * 205) >> 10
    wire = wire - band * WIRES
    column = (wire * 1639) >> 16
    wire = wire - column * COLS
    pair = wire >> 1
    part = jnp.where(pair >= COLS // 4, 1, 0)
    row = (apa & 1) * WIRES + part * (WIRES // 2) + (wire & 1) * (WIRES // 4)
    row = row + (pair - part * (COLS // 4)) * 16 + column
    source = jnp.where(usable, (apa >> 1) * BANDS + band, 255).astype(F32)
    fields[0:PLACES, :] = ((row >> 7) + 1).astype(F32)
    fields[16 : 16 + PLACES, :] = (row & 127).astype(F32)
    block = BLOBS // 3
    upper[0 : 2 * block, :] = jnp.ones((2 * block, block), BF)
    upper[2 * block :, :] = (
        (iota((block, block), 0) < iota((block, block), 1)).astype(F32).astype(BF)
    )
    group = iota((GROUPS, BLOBS), 0).astype(F32).astype(BF)
    for k in range(PLACES):
        hots[k * GROUPS : (k + 1) * GROUPS, :] = one_if(group == tall(source[k : k + 1], GROUPS))
    for j in range(3):
        counts[:, j * block : (j + 1) * block] = dot(
            hots[:, 0 : (j + 1) * block], upper[(2 - j) * block :, :]
        )


def make_requests(fields, request, bslot, hots, counts):
    blob = iota((1, BLOBS), 1)
    blob_high = tall(((blob >> 7) + 1).astype(F32), GROUPS)
    blob_low = tall((blob & 127).astype(F32), GROUPS)
    slot = iota((SLOTS, BLOBS), 0).astype(F32).astype(BF)
    before = jnp.zeros((GROUPS, 1), F32)
    table = jnp.zeros((4 * GROUPS, SLOTS), F32)
    for k in range(PLACES):
        here = slice(k * GROUPS, (k + 1) * GROUPS)
        hot = hots[here, :]
        hot32 = hot.astype(F32)
        count = counts[here, :]
        rank = jnp.sum(hot32 * (count + before), axis=0, keepdims=True)
        before = before + (count + hot32)[:, BLOBS - 1 : BLOBS]
        slot_hot = one_if(slot == tall(rank, SLOTS))
        values = jnp.concatenate(
            [
                hot * tall(fields[k : k + 1, :], GROUPS),
                hot * tall(fields[16 + k : 17 + k, :], GROUPS),
                hot * blob_high,
                hot * blob_low,
            ],
            axis=0,
        )
        table = table + lax.dot_general(
            values, slot_hot, (((1,), (1,)), ((), ())), preferred_element_type=F32
        )
    request[...] = jnp.transpose(table[0 : 2 * GROUPS]).astype(BF)
    bslot[...] = table[2 * GROUPS :]


def pick(reqbox, held, picks, slot, plane, core, band):
    group = plane * 8 + core * BANDS + band
    index = iota((LANES, 2 * LANES), 0)
    choose = index == jnp.where(iota((LANES, 2 * LANES), 1) < LANES, group, group + GROUPS)
    choose = choose.astype(F32).astype(BF)
    height = PICK_OWNERS * SLOTS
    lane = iota((height, LANES), 1).astype(F32).astype(BF)

    def one(n, carry):
        at = pl.ds(PICK_OWNERS * n, PICK_OWNERS)
        asked = reqbox[at].reshape(height, LANES)
        wide = dot(asked, choose)
        high = wide[:, 0:LANES].astype(BF)
        low = one_if(wide[:, LANES:].astype(BF) == lane)
        tiles = [
            jnp.where(high == jnp.asarray(t + 1, BF), low, jnp.zeros((), BF))
            for t in range(2 * WIRES // LANES)
        ]
        got = dot(jnp.concatenate(tiles, axis=1), held[slot])
        picks[slot, at] = got.astype(BF).reshape(PICK_OWNERS, SLOTS, SLICES)
        return carry

    lax.fori_loop(0, PEERS // PICK_OWNERS, one, 0)


def place(bslot, picks, inbox, total, slot, plane, core, band):
    highs = []
    lows = []
    blocks = []
    blob = iota((SLOTS, LANES), 0).astype(F32).astype(BF)
    for r in range(PEERS):
        dc, dy = divmod(r, BANDS)
        from_core = lax.rem(core + dc, 2)
        from_band = lax.rem(band + BANDS - dy, BANDS)
        group = plane * 8 + from_core * BANDS + from_band
        highs.append(tall(bslot[pl.ds(group, 1), :], SLOTS))
        lows.append(one_if(blob == tall(bslot[pl.ds(group + GROUPS, 1), :], SLOTS)))
        blocks.append(picks[slot, 0] if r == 0 else inbox[slot, r])
    incoming = jnp.concatenate(blocks, axis=0)
    high = jnp.concatenate(highs, axis=1)
    low = jnp.concatenate(lows, axis=1)
    hot = jnp.concatenate(
        [
            jnp.where(high == jnp.asarray(m + 1, BF), low, jnp.zeros((), BF))
            for m in range(BLOBS // LANES)
        ],
        axis=0,
    )
    total[...] = total[...] + dot(hot, incoming)


def whole(
    raw_ref, mask_ref, k_ref, wires_ref, sig_ref, blob_ref,
    mask_v, k_v, wires_v, clean, xf, xi, tab, k32, mask8, so, waves, pair_sum, sig_v, held, fields, hots, counts, upper, request, bslot,
    reqbox, picks, inbox,
    halo_send, halo_recv, req_send, req_recv, ring_send, ring_recv, box_send, box_recv, out_sem,
):
    raw_v = sig_v
    fetches = [
        pltpu.make_async_copy(mask_ref, mask_v, out_sem.at[2]),
        pltpu.make_async_copy(raw_ref.at[0], raw_v.at[0], out_sem.at[3]),
        pltpu.make_async_copy(raw_ref.at[1], raw_v.at[1], out_sem.at[4]),
        pltpu.make_async_copy(k_ref, k_v, out_sem.at[5]),
        pltpu.make_async_copy(wires_ref, wires_v, out_sem.at[6]),
    ]
    for fetch in fetches:
        fetch.start()
    apa = lax.axis_index("apa")
    slab = lax.axis_index("slab")
    band = lax.axis_index("band")
    plane = lax.div(apa, 2)
    core = lax.rem(apa, 2)

    def device(dz=0, dc=0, dx=0, dy=0):
        z = lax.rem(plane + dz + PLANES, PLANES)
        c = lax.rem(core + dc, 2)
        return (z * 2 + c, lax.rem(slab + dx + SLABS, SLABS), lax.rem(band + dy + BANDS, BANDS))

    peers = [device(dc=r // BANDS, dy=r % BANDS) for r in range(PEERS)]
    everyone = peers[1:] + [device(dz=1), device(dz=-1), device(dx=1), device(dx=-1)]
    everyone += [device(dx=i, dy=j) for i in (-1, 1) for j in (-1, 1)]
    barrier = pltpu.get_barrier_semaphore()
    for other in everyone:
        pl.semaphore_signal(barrier, inc=1, device_id=other, device_id_type=MESH)

    mask8[...] = jnp.zeros_like(mask8)
    fetches[0].wait()
    mask8[0:2, :] = mask_v[...].astype(F32)
    live = jnp.transpose(mask8[...])

    def remote(src, dst, send, recv, to):
        return pltpu.make_async_remote_copy(
            src_ref=src, dst_ref=dst, send_sem=send, recv_sem=recv, device_id=to, device_id_type=MESH
        )

    own = slice(EDGE, EDGE + WIRES)
    mid = slice(H, H + TICKS)
    row_parts = {
        -1: (slice(EDGE, 2 * EDGE), slice(EDGE + WIRES, TALL)),
        0: (own, own),
        1: (slice(WIRES, EDGE + WIRES), slice(0, EDGE)),
    }
    col_parts = {
        -1: (slice(H, 2 * H), slice(H + TICKS, LONG)),
        0: (mid, mid),
        1: (slice(2 * H, 3 * H), slice(0, H)),
    }
    halos = {0: [], 1: []}
    number = 0
    for ap in range(2):
        fetches[1 + ap].wait()
        mask_waves(raw_v, live, clean, ap)
        if ap == 0:
            fetches[3].wait()
            build_tables(k_v, k32, tab)
            pl.semaphore_wait(barrier, len(everyone))
        for dx in (-1, 1, 0):
            for dy in (-1, 0, 1):
                if dx == 0 and dy == 0:
                    continue
                (rs, rd), (cs, cd) = row_parts[dy], col_parts[dx]
                copy = remote(
                    clean.at[ap, rs, cs], clean.at[ap, rd, cd],
                    halo_send.at[number], halo_recv.at[number], device(dx=dx, dy=dy),
                )
                copy.start()
                halos[ap].append(copy)
                number += 1

    pair_hit = (iota((TICKS, SLICES), 0) >> 1) == iota((TICKS, SLICES), 1)
    pair_sum[...] = pair_hit.astype(F32).astype(BF)
    fetches[4].wait()
    count_places(wires_v, fields, hots, counts, upper)
    make_requests(fields, request, bslot, hots, counts)
    reqbox[0] = request[...]
    asks = []
    for r in range(1, PEERS):
        dc, dy = divmod(r, BANDS)
        back = dc * BANDS + (BANDS - dy) % BANDS
        copy = remote(request, reqbox.at[back], req_send.at[back], req_recv.at[back], peers[r])
        copy.start()
        asks.append(copy)
    has = (slab > 0, slab < SLABS - 1, band > 0, band < BANDS - 1)

    towards = (device(dz=1), device(dz=-1))
    quarter = WIRES // PARTS

    def slot_at(way, distance):
        if distance == 0:
            return 0
        if distance == 4:
            return 7
        return distance + 3 * way

    def ring(way, distance, piece):
        if distance == 1:
            number, rows = piece, slice(piece * quarter, (piece + 1) * quarter)
        else:
            number = 4 + 2 * (distance - 2) + (piece if distance < 4 else 0)
            rows = slice(piece * WIRES, (piece + 1) * WIRES)
        return remote(
            held.at[slot_at(way, distance - 1), rows],
            held.at[slot_at(way, distance), rows],
            ring_send.at[way, number], ring_recv.at[way, number], towards[way],
        )

    writes = []
    started = []
    def start(copy):
        copy.start()
        started.append(copy)

    def forward(distance, half):
        for way in range(2):
            if distance == 1:
                for part in range(PARTS):
                    ring(way, 1, half * PARTS + part).wait_recv()
            else:
                ring(way, distance, half).wait_recv()
            if distance < 3 or half == way:
                start(ring(way, distance + 1, half))

    def receive(ap):
        for copy in halos[ap]:
            copy.wait_recv()
        interleave(clean, xf, xi, ap, has)

    def advance(ap, part):
        convolve(xi, tab, so.at[ap], waves, held, pair_sum, ap, part)
        for way in range(2):
            start(ring(way, 1, ap * PARTS + part))

    receive(0)
    advance(0, 0)
    advance(0, 1)
    receive(1)
    advance(1, 0)
    advance(1, 1)

    def write_signal(ap):
        sig_v[ap] = jnp.concatenate([so[ap, t] for t in range(TICKS // LANES)], axis=1).astype(BF)
        write = pltpu.make_async_copy(sig_v.at[ap], sig_ref.at[ap], out_sem.at[ap])
        write.start()
        writes.append(write)

    boxes = {}

    def serve(slot, shift):
        source = lax.rem(plane + shift + PLANES, PLANES)
        pick(reqbox, held, picks, slot, source, core, band)
        boxes[slot] = []
        for r in range(1, PEERS):
            copy = remote(
                picks.at[slot, r], inbox.at[slot, r], box_send.at[slot, r], box_recv.at[slot, r], peers[r]
            )
            copy.start()
            boxes[slot].append(copy)

    def collect(slot, shift):
        source = lax.rem(plane + shift + PLANES, PLANES)
        for copy in boxes[slot]:
            copy.wait_recv()
        place(bslot, picks, inbox, blob_ref, slot, source, core, band)

    forward(1, 0)
    for copy in asks:
        copy.wait_recv()
    serve(0, 0)
    forward(1, 1)
    serve(1, -1)
    serve(4, 1)
    write_signal(0)
    forward(2, 0)
    write_signal(1)
    blob_ref[...] = jnp.zeros_like(blob_ref)
    collect(0, 0)
    forward(2, 1)
    serve(2, -2)
    serve(5, 2)
    collect(1, -1)
    collect(4, 1)
    forward(3, 0)
    forward(3, 1)
    serve(3, -3)
    serve(6, 3)
    collect(2, -2)
    ring(0, 4, 0).wait_recv()
    ring(1, 4, 1).wait_recv()
    serve(7, 4)
    collect(5, 2)
    collect(3, -3)
    collect(6, 3)
    collect(7, 4)

    for copies in (halos[0], halos[1], asks, started, *boxes.values()):
        for copy in copies:
            copy.wait_send()
    for write in writes:
        write.wait()


def hand_over(signal, charge):
    def body(signal_in, charge_in, signal_out, charge_out):
        signal_out[...] = signal_in[...]
        charge_out[...] = charge_in[...]

    steps = 2
    wave = pl.BlockSpec((2 // steps, WIRES, TICKS), lambda i: (i, 0, 0))
    blob = pl.BlockSpec((BLOBS // steps, SLICES), lambda i: (i, 0))
    return pl.pallas_call(
        body,
        grid=(steps,),
        out_shape=tuple(jax.ShapeDtypeStruct(x.shape, x.dtype) for x in (signal, charge)),
        in_specs=[wave, blob],
        out_specs=(wave, blob),
    )(signal, charge)


def shards(raw, dead_mask, kernel, blob_wires):
    vmem = pl.BlockSpec(memory_space=pltpu.VMEM)
    dma = pltpu.SemaphoreType.DMA
    signal, charge = pl.pallas_call(
        whole,
        out_shape=(
            jax.ShapeDtypeStruct((2, WIRES, TICKS), BF),
            jax.ShapeDtypeStruct((BLOBS, SLICES), F32),
        ),
        in_specs=[pl.BlockSpec(memory_space=pl.ANY)] * 4,
        out_specs=(pl.BlockSpec(memory_space=pl.ANY), vmem),
        scratch_shapes=[
            pltpu.VMEM((2, WIRES), jnp.int32),
            pltpu.VMEM((TAPS, TICKS + 1), BF),
            pltpu.VMEM((PLACES, BLOBS), jnp.int32),
            pltpu.VMEM((2, TALL, LONG), BF),
            pltpu.VMEM((LONG // LANES, TALL, LANES), F32),
            pltpu.VMEM((2, COLS // 2 + WR, 2, 2, 16, REACH), BF),
            pltpu.VMEM((TAPS + 1, REACH, TICKS), BF),
            pltpu.VMEM((24, LONG), F32),
            pltpu.VMEM((8, WIRES), F32),
            pltpu.VMEM((2, TICKS // LANES, WIRES, LANES), F32),
            pltpu.VMEM((WIRES // PARTS, TICKS), BF),
            pltpu.VMEM((TICKS, SLICES), BF),
            pltpu.VMEM((2, WIRES, TICKS), BF),
            pltpu.VMEM((PLANES, 2 * WIRES, SLICES), BF),
            pltpu.VMEM((32, BLOBS), F32),
            pltpu.VMEM((PLACES * GROUPS, BLOBS), BF),
            pltpu.VMEM((PLACES * GROUPS, BLOBS), F32),
            pltpu.VMEM((BLOBS, BLOBS // 3), BF),
            pltpu.VMEM((SLOTS, LANES), BF),
            pltpu.VMEM((LANES, SLOTS), F32),
            pltpu.VMEM((PEERS, SLOTS, LANES), BF),
            pltpu.VMEM((PLANES, PEERS, SLOTS, SLICES), BF),
            pltpu.VMEM((PLANES, PEERS, SLOTS, SLICES), BF),
            dma((16,)),
            dma((16,)),
            dma((PEERS,)),
            dma((PEERS,)),
            dma((2, 9)),
            dma((2, 9)),
            dma((PLANES, PEERS)),
            dma((PLANES, PEERS)),
            dma((7,)),
        ],
        compiler_params=pltpu.CompilerParams(
            collective_id=0, has_side_effects=True, vmem_limit_bytes=56 << 20
        ),
    )(raw, dead_mask, kernel, blob_wires.T)
    return hand_over(signal, charge)


def solution(mesh):
    return jax.shard_map(
        shards,
        mesh=mesh,
        in_specs=(P("apa", "band", "slab"), P("apa", "band"), P(), P(("apa", "band"), None)),
        out_specs=(P("apa", "band", "slab"), P(("apa", "band"), "slab")),
        check_vma=False,
    )
```

```python
import jax
import jax.numpy as jnp
from jax import lax
from jax.experimental import pallas as pl
from jax.experimental.pallas import tpu as pltpu
from jax.sharding import PartitionSpec as P

W = 2560
WR = 10
H = 128
TAPS = 2 * WR + 1
BANDS = 4
SLABS = 4
PLANES = 8
PEERS = 8
WIRES = W // BANDS
TICKS = 2 * H
LONG = 2 * TICKS
REACH = 3 * H
EDGE = 16
TALL = WIRES + 2 * EDGE
SLICES = TICKS // 2
SLOTS = 128
BLOBS = 768
PLACES = 12
COLS = 40
LANES = 128
GROUPS = 64
PICK_OWNERS = 8
PARTS = 2
CONV_GROUPS = tuple((u, u + 2) for u in range(0, 22, 2))
BF = jnp.bfloat16
F32 = jnp.float32
MESH = pl.DeviceIdType.MESH


def iota(shape, dim):
    return lax.broadcasted_iota(jnp.int32, shape, dim)


def dot(a, b):
    return jnp.dot(a, b, preferred_element_type=F32)


def build_tables(k_ref, k32, tab):
    k32[...] = jnp.zeros_like(k32)
    k32[0:TAPS, 0 : TICKS + 1] = k_ref[...].astype(F32)
    source = iota((H, H), 0)
    target = iota((H, H), 1)
    nothing = jnp.zeros((REACH, H), BF)
    tab[0, :, H:TICKS] = nothing
    tab[TAPS, :, 0:H] = nothing

    def one(p, carry):
        row = k32[pl.ds(p, 1), 0:TICKS]

        def turned(start):
            piece = jnp.broadcast_to(row[:, start : start + H], (H, H))
            return pltpu.roll(piece, 0, 1, stride=1, stride_axis=0)

        last = k32[pl.ds(p, 1), TICKS:LONG][:, 0:1]
        early, late = turned(0), turned(H)
        first = jnp.where(source > target, late, jnp.where(target == source, last, 0.0)).astype(BF)
        second = jnp.where(target >= source, late, early).astype(BF)
        third = jnp.where(target >= source, early, 0.0).astype(BF)
        for n, part in enumerate((first, second, third)):
            tab[p, n * H : (n + 1) * H, 0:H] = part
            tab[p + 1, n * H : (n + 1) * H, H:TICKS] = part
        return carry

    lax.fori_loop(0, TAPS, one, 0, unroll=TAPS)


def mask_waves(raw, live, clean, ap):
    wave = raw[ap].astype(F32) * live[:, ap : ap + 1]
    clean[ap, EDGE : EDGE + WIRES, H : H + TICKS] = wave.astype(BF)


def interleave(clean, xf, xi, ap, has):
    left, right, above, below = has
    rows = ((0, EDGE, above), (EDGE, EDGE + WIRES, None), (EDGE + WIRES, TALL, below))
    cols = ((0, H, left), (H, H + TICKS, None), (H + TICKS, LONG, right))
    for r0, r1, row_ok in rows:
        for c0, c1, col_ok in cols:
            part = clean[ap, r0:r1, c0:c1].astype(F32)
            if row_ok is not None:
                part = jnp.where(row_ok, part, 0.0)
            if col_ok is not None:
                part = jnp.where(col_ok, part, 0.0)
            for t in range((c1 - c0) // LANES):
                xf[c0 // LANES + t, r0:r1, :] = part[:, t * LANES : (t + 1) * LANES]
    first = EDGE - WR

    def one(i, carry):
        for t in range(LONG // LANES):
            picked = xf[t, pl.ds(i + first, 16, stride=COLS), :]
            picked = picked.astype(BF)
            if t < 3:
                xi[ap, lax.div(i, 2), lax.rem(i, 2), 0, :, t * LANES : (t + 1) * LANES] = picked
            if t > 0:
                xi[ap, lax.div(i, 2), lax.rem(i, 2), 1, :, (t - 1) * LANES : t * LANES] = picked
        return carry

    lax.fori_loop(0, COLS + 2 * WR, one, 0, unroll=COLS + 2 * WR)


def convolve(xi, tab, so, waves, held, pair_sum, ap, part):
    pairs = COLS // (2 * PARTS)
    first = part * pairs
    total = None
    for u0, u1 in CONV_GROUPS:
        pieces = [
            xi[ap, first + u // 2 : first + u // 2 + pairs, u % 2].reshape(pairs * 32, REACH)
            for u in range(u0, u1)
        ]
        rhs = tab[u0:u1].reshape((u1 - u0) * REACH, TICKS)
        term = dot(jnp.concatenate(pieces, axis=1), rhs)
        total = term if total is None else total + term
    rows = pairs * 16
    total = total.reshape(pairs, 2, 16, TICKS)
    for n in range(2):
        ends = [total[:, tb, :, n * H : (n + 1) * H].reshape(rows, H) for tb in range(2)]
        for tb, end in enumerate(ends):
            waves[n * rows : (n + 1) * rows, tb * H : (tb + 1) * H] = end.astype(BF)
            for i in range(pairs):
                wire = 2 * (first + i) + n
                so[tb, pl.ds(wire, 16, stride=COLS), :] = end[16 * i : 16 * (i + 1)]
    start = (ap * PARTS + part) * 2 * rows

    def pairwise(n, carry):
        at = pl.ds(pl.multiple_of(n * rows, rows), rows)
        to = pl.ds(pl.multiple_of(start + n * rows, rows), rows)
        held[0, to, :] = dot(waves[at, :], pair_sum[...]).astype(BF)
        return carry

    lax.fori_loop(0, 2, pairwise, 0)


def tall(row, height):
    block = jnp.broadcast_to(row, (16, row.shape[1])).astype(BF)
    return jnp.concatenate([block] * (height // 16), axis=0)


def one_if(hit):
    return jnp.where(hit, jnp.ones((), BF), jnp.zeros((), BF))


def count_places(wires_ref, fields, hots, counts, upper):
    refs = wires_ref[...]
    usable = refs >= 0
    wire = jnp.where(usable, refs, 0)
    apa = ((wire >> 9) * 205) >> 10
    wire = wire - apa * W
    band = ((wire >> 7) * 205) >> 10
    wire = wire - band * WIRES
    column = (wire * 1639) >> 16
    wire = wire - column * COLS
    pair = wire >> 1
    part = jnp.where(pair >= COLS // 4, 1, 0)
    row = (apa & 1) * WIRES + part * (WIRES // 2) + (wire & 1) * (WIRES // 4)
    row = row + (pair - part * (COLS // 4)) * 16 + column
    source = jnp.where(usable, (apa >> 1) * BANDS + band, 255).astype(F32)
    fields[0:PLACES, :] = ((row >> 7) + 1).astype(F32)
    fields[16 : 16 + PLACES, :] = (row & 127).astype(F32)
    block = BLOBS // 3
    upper[0 : 2 * block, :] = jnp.ones((2 * block, block), BF)
    upper[2 * block :, :] = (
        (iota((block, block), 0) < iota((block, block), 1)).astype(F32).astype(BF)
    )
    group = iota((GROUPS, BLOBS), 0).astype(F32).astype(BF)
    for k in range(PLACES):
        hots[k * GROUPS : (k + 1) * GROUPS, :] = one_if(group == tall(source[k : k + 1], GROUPS))
    for j in range(3):
        counts[:, j * block : (j + 1) * block] = dot(
            hots[:, 0 : (j + 1) * block], upper[(2 - j) * block :, :]
        )


def make_requests(fields, request, bslot, hots, counts):
    blob = iota((1, BLOBS), 1)
    blob_high = ((blob >> 7) + 1).astype(F32)
    blob_low = tall((blob & 127).astype(F32), GROUPS)
    slot = iota((SLOTS, BLOBS), 0).astype(F32).astype(BF)
    before = jnp.zeros((GROUPS, 1), F32)
    table = jnp.zeros((3 * GROUPS, SLOTS), F32)
    for k in range(PLACES):
        here = slice(k * GROUPS, (k + 1) * GROUPS)
        hot = hots[here, :]
        hot32 = hot.astype(F32)
        count = counts[here, :]
        rank = jnp.sum(hot32 * (count + before), axis=0, keepdims=True)
        before = before + (count + hot32)[:, BLOBS - 1 : BLOBS]
        slot_hot = one_if(slot == tall(rank, SLOTS))
        values = jnp.concatenate(
            [
                hot * tall(fields[k : k + 1, :] * 8.0 + blob_high, GROUPS),
                hot * tall(fields[16 + k : 17 + k, :], GROUPS),
                hot * blob_low,
            ],
            axis=0,
        )
        table = table + lax.dot_general(
            values, slot_hot, (((1,), (1,)), ((), ())), preferred_element_type=F32
        )
    both = table[0:GROUPS].astype(jnp.int32)
    row_high = (both >> 3).astype(F32)
    request[...] = jnp.transpose(
        jnp.concatenate([row_high, table[GROUPS : 2 * GROUPS]], axis=0)
    ).astype(BF)
    bslot[0:GROUPS, :] = (both & 7).astype(F32)
    bslot[GROUPS:, :] = table[2 * GROUPS :]


def pick(reqbox, held, picks, slot, plane, core, band):
    group = plane * 8 + core * BANDS + band
    index = iota((LANES, 2 * LANES), 0)
    choose = index == jnp.where(iota((LANES, 2 * LANES), 1) < LANES, group, group + GROUPS)
    choose = choose.astype(F32).astype(BF)
    height = PICK_OWNERS * SLOTS
    lane = iota((height, LANES), 1).astype(F32).astype(BF)

    def one(n, carry):
        at = pl.ds(PICK_OWNERS * n, PICK_OWNERS)
        asked = reqbox[at].reshape(height, LANES)
        wide = dot(asked, choose)
        high = wide[:, 0:LANES].astype(BF)
        low = one_if(wide[:, LANES:].astype(BF) == lane)
        tiles = [
            jnp.where(high == jnp.asarray(t + 1, BF), low, jnp.zeros((), BF))
            for t in range(2 * WIRES // LANES)
        ]
        got = dot(jnp.concatenate(tiles, axis=1), held[slot])
        picks[slot, at] = got.astype(BF).reshape(PICK_OWNERS, SLOTS, SLICES)
        return carry

    lax.fori_loop(0, PEERS // PICK_OWNERS, one, 0)


def place(bslot, picks, inbox, total, slot, plane, core, band):
    highs = []
    lows = []
    blocks = []
    blob = iota((SLOTS, LANES), 0).astype(F32).astype(BF)
    for r in range(PEERS):
        dc, dy = divmod(r, BANDS)
        from_core = lax.rem(core + dc, 2)
        from_band = lax.rem(band + BANDS - dy, BANDS)
        group = plane * 8 + from_core * BANDS + from_band
        highs.append(tall(bslot[pl.ds(group, 1), :], SLOTS))
        lows.append(one_if(blob == tall(bslot[pl.ds(group + GROUPS, 1), :], SLOTS)))
        blocks.append(picks[slot, 0] if r == 0 else inbox[slot, r])
    incoming = jnp.concatenate(blocks, axis=0)
    high = jnp.concatenate(highs, axis=1)
    low = jnp.concatenate(lows, axis=1)
    hot = jnp.concatenate(
        [
            jnp.where(high == jnp.asarray(m + 1, BF), low, jnp.zeros((), BF))
            for m in range(BLOBS // LANES)
        ],
        axis=0,
    )
    total[...] = total[...] + dot(hot, incoming)


def whole(
    raw_ref, mask_ref, k_ref, wires_ref, sig_ref, blob_ref,
    mask_v, k_v, wires_v, clean, xf, xi, tab, k32, mask8, so, waves, pair_sum, sig_v, held, fields, hots, counts, upper, request, bslot,
    reqbox, picks, inbox,
    halo_send, halo_recv, req_send, req_recv, ring_send, ring_recv, box_send, box_recv, out_sem,
):
    raw_v = sig_v
    fetches = [
        pltpu.make_async_copy(mask_ref, mask_v, out_sem.at[2]),
        pltpu.make_async_copy(raw_ref.at[0], raw_v.at[0], out_sem.at[3]),
        pltpu.make_async_copy(raw_ref.at[1], raw_v.at[1], out_sem.at[4]),
        pltpu.make_async_copy(k_ref, k_v, out_sem.at[5]),
        pltpu.make_async_copy(wires_ref, wires_v, out_sem.at[6]),
    ]
    for fetch in fetches:
        fetch.start()
    apa = lax.axis_index("apa")
    slab = lax.axis_index("slab")
    band = lax.axis_index("band")
    plane = lax.div(apa, 2)
    core = lax.rem(apa, 2)

    def device(dz=0, dc=0, dx=0, dy=0):
        z = lax.rem(plane + dz + PLANES, PLANES)
        c = lax.rem(core + dc, 2)
        return (z * 2 + c, lax.rem(slab + dx + SLABS, SLABS), lax.rem(band + dy + BANDS, BANDS))

    peers = [device(dc=r // BANDS, dy=r % BANDS) for r in range(PEERS)]
    everyone = peers[1:] + [device(dz=1), device(dz=-1), device(dx=1), device(dx=-1)]
    everyone += [device(dx=i, dy=j) for i in (-1, 1) for j in (-1, 1)]
    barrier = pltpu.get_barrier_semaphore()
    for other in everyone:
        pl.semaphore_signal(barrier, inc=1, device_id=other, device_id_type=MESH)

    mask8[...] = jnp.zeros_like(mask8)
    fetches[0].wait()
    mask8[0:2, :] = mask_v[...].astype(F32)
    live = jnp.transpose(mask8[...])

    def remote(src, dst, send, recv, to):
        return pltpu.make_async_remote_copy(
            src_ref=src, dst_ref=dst, send_sem=send, recv_sem=recv, device_id=to, device_id_type=MESH
        )

    own = slice(EDGE, EDGE + WIRES)
    mid = slice(H, H + TICKS)
    row_parts = {
        -1: (slice(EDGE, 2 * EDGE), slice(EDGE + WIRES, TALL)),
        0: (own, own),
        1: (slice(WIRES, EDGE + WIRES), slice(0, EDGE)),
    }
    col_parts = {
        -1: (slice(H, 2 * H), slice(H + TICKS, LONG)),
        0: (mid, mid),
        1: (slice(2 * H, 3 * H), slice(0, H)),
    }
    halos = {0: [], 1: []}
    number = 0
    for ap in range(2):
        fetches[1 + ap].wait()
        mask_waves(raw_v, live, clean, ap)
        if ap == 0:
            fetches[3].wait()
            build_tables(k_v, k32, tab)
            pl.semaphore_wait(barrier, len(everyone))
        for dx in (-1, 1, 0):
            for dy in (-1, 0, 1):
                if dx == 0 and dy == 0:
                    continue
                (rs, rd), (cs, cd) = row_parts[dy], col_parts[dx]
                copy = remote(
                    clean.at[ap, rs, cs], clean.at[ap, rd, cd],
                    halo_send.at[number], halo_recv.at[number], device(dx=dx, dy=dy),
                )
                copy.start()
                halos[ap].append(copy)
                number += 1

    pair_hit = (iota((TICKS, SLICES), 0) >> 1) == iota((TICKS, SLICES), 1)
    pair_sum[...] = pair_hit.astype(F32).astype(BF)
    fetches[4].wait()
    count_places(wires_v, fields, hots, counts, upper)
    make_requests(fields, request, bslot, hots, counts)
    reqbox[0] = request[...]
    asks = []
    for r in range(1, PEERS):
        dc, dy = divmod(r, BANDS)
        back = dc * BANDS + (BANDS - dy) % BANDS
        copy = remote(request, reqbox.at[back], req_send.at[back], req_recv.at[back], peers[r])
        copy.start()
        asks.append(copy)
    has = (slab > 0, slab < SLABS - 1, band > 0, band < BANDS - 1)

    towards = (device(dz=1), device(dz=-1))
    quarter = WIRES // PARTS

    def slot_at(way, distance):
        if distance == 0:
            return 0
        if distance == 4:
            return 7
        return distance + 3 * way

    def ring(way, distance, piece):
        if distance == 1:
            number, rows = piece, slice(piece * quarter, (piece + 1) * quarter)
        else:
            number = 4 + 2 * (distance - 2) + (piece if distance < 4 else 0)
            rows = slice(piece * WIRES, (piece + 1) * WIRES)
        return remote(
            held.at[slot_at(way, distance - 1), rows],
            held.at[slot_at(way, distance), rows],
            ring_send.at[way, number], ring_recv.at[way, number], towards[way],
        )

    writes = []
    started = []
    def start(copy):
        copy.start()
        started.append(copy)

    def forward(distance, half):
        for way in range(2):
            if distance == 1:
                for part in range(PARTS):
                    ring(way, 1, half * PARTS + part).wait_recv()
            else:
                ring(way, distance, half).wait_recv()
            if distance < 3 or half == way:
                start(ring(way, distance + 1, half))

    def receive(ap):
        for copy in halos[ap]:
            copy.wait_recv()
        interleave(clean, xf, xi, ap, has)

    def advance(ap, part):
        convolve(xi, tab, so.at[ap], waves, held, pair_sum, ap, part)
        for way in range(2):
            start(ring(way, 1, ap * PARTS + part))

    receive(0)
    advance(0, 0)
    advance(0, 1)
    receive(1)
    advance(1, 0)
    advance(1, 1)

    def write_signal(ap):
        sig_v[ap] = jnp.concatenate([so[ap, t] for t in range(TICKS // LANES)], axis=1).astype(BF)
        write = pltpu.make_async_copy(sig_v.at[ap], sig_ref.at[ap], out_sem.at[ap])
        write.start()
        writes.append(write)

    boxes = {}

    def serve(slot, shift):
        source = lax.rem(plane + shift + PLANES, PLANES)
        pick(reqbox, held, picks, slot, source, core, band)
        boxes[slot] = []
        for r in (2, 6, 1, 3, 5, 7, 4):
            copy = remote(
                picks.at[slot, r], inbox.at[slot, r], box_send.at[slot, r], box_recv.at[slot, r], peers[r]
            )
            copy.start()
            boxes[slot].append(copy)

    def collect(slot, shift):
        source = lax.rem(plane + shift + PLANES, PLANES)
        for copy in boxes[slot]:
            copy.wait_recv()
        place(bslot, picks, inbox, blob_ref, slot, source, core, band)

    forward(1, 0)
    for copy in asks:
        copy.wait_recv()
    serve(0, 0)
    forward(1, 1)
    serve(1, -1)
    serve(4, 1)
    write_signal(0)
    forward(2, 0)
    write_signal(1)
    blob_ref[...] = jnp.zeros_like(blob_ref)
    collect(0, 0)
    forward(2, 1)
    serve(2, -2)
    serve(5, 2)
    collect(1, -1)
    collect(4, 1)
    forward(3, 0)
    forward(3, 1)
    serve(3, -3)
    serve(6, 3)
    collect(2, -2)
    ring(0, 4, 0).wait_recv()
    ring(1, 4, 1).wait_recv()
    serve(7, 4)
    collect(5, 2)
    collect(3, -3)
    collect(6, 3)
    collect(7, 4)

    for copies in (halos[0], halos[1], asks, started, *boxes.values()):
        for copy in copies:
            copy.wait_send()
    for write in writes:
        write.wait()


def hand_over(signal, charge):
    def body(signal_in, charge_in, signal_out, charge_out):
        signal_out[...] = signal_in[...]
        charge_out[...] = charge_in[...]

    steps = 2
    wave = pl.BlockSpec((2 // steps, WIRES, TICKS), lambda i: (i, 0, 0))
    blob = pl.BlockSpec((BLOBS // steps, SLICES), lambda i: (i, 0))
    return pl.pallas_call(
        body,
        grid=(steps,),
        out_shape=tuple(jax.ShapeDtypeStruct(x.shape, x.dtype) for x in (signal, charge)),
        in_specs=[wave, blob],
        out_specs=(wave, blob),
    )(signal, charge)


def shards(raw, dead_mask, kernel, blob_wires):
    vmem = pl.BlockSpec(memory_space=pltpu.VMEM)
    dma = pltpu.SemaphoreType.DMA
    signal, charge = pl.pallas_call(
        whole,
        out_shape=(
            jax.ShapeDtypeStruct((2, WIRES, TICKS), BF),
            jax.ShapeDtypeStruct((BLOBS, SLICES), F32),
        ),
        in_specs=[pl.BlockSpec(memory_space=pl.ANY)] * 4,
        out_specs=(pl.BlockSpec(memory_space=pl.ANY), vmem),
        scratch_shapes=[
            pltpu.VMEM((2, WIRES), jnp.int32),
            pltpu.VMEM((TAPS, TICKS + 1), BF),
            pltpu.VMEM((PLACES, BLOBS), jnp.int32),
            pltpu.VMEM((2, TALL, LONG), BF),
            pltpu.VMEM((LONG // LANES, TALL, LANES), F32),
            pltpu.VMEM((2, COLS // 2 + WR, 2, 2, 16, REACH), BF),
            pltpu.VMEM((TAPS + 1, REACH, TICKS), BF),
            pltpu.VMEM((24, LONG), F32),
            pltpu.VMEM((8, WIRES), F32),
            pltpu.VMEM((2, TICKS // LANES, WIRES, LANES), F32),
            pltpu.VMEM((WIRES // PARTS, TICKS), BF),
            pltpu.VMEM((TICKS, SLICES), BF),
            pltpu.VMEM((2, WIRES, TICKS), BF),
            pltpu.VMEM((PLANES, 2 * WIRES, SLICES), BF),
            pltpu.VMEM((32, BLOBS), F32),
            pltpu.VMEM((PLACES * GROUPS, BLOBS), BF),
            pltpu.VMEM((PLACES * GROUPS, BLOBS), F32),
            pltpu.VMEM((BLOBS, BLOBS // 3), BF),
            pltpu.VMEM((SLOTS, LANES), BF),
            pltpu.VMEM((LANES, SLOTS), F32),
            pltpu.VMEM((PEERS, SLOTS, LANES), BF),
            pltpu.VMEM((PLANES, PEERS, SLOTS, SLICES), BF),
            pltpu.VMEM((PLANES, PEERS, SLOTS, SLICES), BF),
            dma((16,)),
            dma((16,)),
            dma((PEERS,)),
            dma((PEERS,)),
            dma((2, 9)),
            dma((2, 9)),
            dma((PLANES, PEERS)),
            dma((PLANES, PEERS)),
            dma((7,)),
        ],
        compiler_params=pltpu.CompilerParams(
            collective_id=0, has_side_effects=True, vmem_limit_bytes=56 << 20
        ),
    )(raw, dead_mask, kernel, blob_wires.T)
    return hand_over(signal, charge)


def solution(mesh):
    return jax.shard_map(
        shards,
        mesh=mesh,
        in_specs=(P("apa", "band", "slab"), P("apa", "band"), P(), P(("apa", "band"), None)),
        out_specs=(P("apa", "band", "slab"), P(("apa", "band"), "slab")),
        check_vma=False,
    )
```

```python
import jax
import jax.numpy as jnp
from jax import lax
from jax.experimental import pallas as pl
from jax.experimental.pallas import tpu as pltpu
from jax.sharding import PartitionSpec as P

W = 2560
WR = 10
H = 128
TAPS = 2 * WR + 1
BANDS = 4
SLABS = 4
PLANES = 8
PEERS = 8
WIRES = W // BANDS
TICKS = 2 * H
LONG = 2 * TICKS
REACH = 3 * H
EDGE = 16
TALL = WIRES + 2 * EDGE
SLICES = TICKS // 2
SLOTS = 128
BLOBS = 768
PLACES = 12
COLS = 40
LANES = 128
GROUPS = 64
PICK_OWNERS = 8
PARTS = 2
CONV_GROUPS = tuple((u, u + 2) for u in range(0, 22, 2))
BF = jnp.bfloat16
F32 = jnp.float32
MESH = pl.DeviceIdType.MESH


def iota(shape, dim):
    return lax.broadcasted_iota(jnp.int32, shape, dim)


def dot(a, b):
    return jnp.dot(a, b, preferred_element_type=F32)


def build_tables(k_ref, k32, tab):
    k32[...] = jnp.zeros_like(k32)
    k32[0:TAPS, 0 : TICKS + 1] = k_ref[...].astype(F32)
    source = iota((H, H), 0)
    target = iota((H, H), 1)
    nothing = jnp.zeros((REACH, H), BF)
    tab[0, :, H:TICKS] = nothing
    tab[TAPS, :, 0:H] = nothing

    def one(p, carry):
        row = k32[pl.ds(p, 1), 0:TICKS]

        def turned(start):
            piece = jnp.broadcast_to(row[:, start : start + H], (H, H))
            return pltpu.roll(piece, 0, 1, stride=1, stride_axis=0)

        last = k32[pl.ds(p, 1), TICKS:LONG][:, 0:1]
        early, late = turned(0), turned(H)
        first = jnp.where(source > target, late, jnp.where(target == source, last, 0.0)).astype(BF)
        second = jnp.where(target >= source, late, early).astype(BF)
        third = jnp.where(target >= source, early, 0.0).astype(BF)
        for n, part in enumerate((first, second, third)):
            tab[p, n * H : (n + 1) * H, 0:H] = part
            tab[p + 1, n * H : (n + 1) * H, H:TICKS] = part
        return carry

    lax.fori_loop(0, TAPS, one, 0, unroll=TAPS)


def mask_waves(raw, live, clean, ap):
    wave = raw[ap].astype(F32) * live[:, ap : ap + 1]
    clean[ap, EDGE : EDGE + WIRES, H : H + TICKS] = wave.astype(BF)


def interleave(clean, xf, xi, ap, has):
    left, right, above, below = has
    rows = ((0, EDGE, above), (EDGE, EDGE + WIRES, None), (EDGE + WIRES, TALL, below))
    cols = ((0, H, left), (H, H + TICKS, None), (H + TICKS, LONG, right))
    for r0, r1, row_ok in rows:
        for c0, c1, col_ok in cols:
            part = clean[ap, r0:r1, c0:c1].astype(F32)
            if row_ok is not None:
                part = jnp.where(row_ok, part, 0.0)
            if col_ok is not None:
                part = jnp.where(col_ok, part, 0.0)
            for t in range((c1 - c0) // LANES):
                xf[c0 // LANES + t, r0:r1, :] = part[:, t * LANES : (t + 1) * LANES]
    first = EDGE - WR

    def one(i, carry):
        for t in range(LONG // LANES):
            picked = xf[t, pl.ds(i + first, 16, stride=COLS), :]
            picked = picked.astype(BF)
            if t < 3:
                xi[ap, lax.div(i, 2), lax.rem(i, 2), 0, :, t * LANES : (t + 1) * LANES] = picked
            if t > 0:
                xi[ap, lax.div(i, 2), lax.rem(i, 2), 1, :, (t - 1) * LANES : t * LANES] = picked
        return carry

    lax.fori_loop(0, COLS + 2 * WR, one, 0, unroll=COLS + 2 * WR)


def convolve(xi, tab, so, waves, held, pair_sum, ap, part):
    pairs = COLS // (2 * PARTS)
    first = part * pairs
    total = None
    for u0, u1 in CONV_GROUPS:
        pieces = [
            xi[ap, first + u // 2 : first + u // 2 + pairs, u % 2].reshape(pairs * 32, REACH)
            for u in range(u0, u1)
        ]
        rhs = tab[u0:u1].reshape((u1 - u0) * REACH, TICKS)
        term = dot(jnp.concatenate(pieces, axis=1), rhs)
        total = term if total is None else total + term
    rows = pairs * 16
    total = total.reshape(pairs, 2, 16, TICKS)
    for n in range(2):
        ends = [total[:, tb, :, n * H : (n + 1) * H].reshape(rows, H) for tb in range(2)]
        for tb, end in enumerate(ends):
            waves[n * rows : (n + 1) * rows, tb * H : (tb + 1) * H] = end.astype(BF)
            for i in range(pairs):
                wire = 2 * (first + i) + n
                so[tb, pl.ds(wire, 16, stride=COLS), :] = end[16 * i : 16 * (i + 1)]
    start = (ap * PARTS + part) * 2 * rows

    def pairwise(n, carry):
        at = pl.ds(pl.multiple_of(n * rows, rows), rows)
        to = pl.ds(pl.multiple_of(start + n * rows, rows), rows)
        held[0, to, :] = dot(waves[at, :], pair_sum[...]).astype(BF)
        return carry

    lax.fori_loop(0, 2, pairwise, 0)


def tall(row, height):
    block = jnp.broadcast_to(row, (16, row.shape[1])).astype(BF)
    return jnp.concatenate([block] * (height // 16), axis=0)


def one_if(hit):
    return jnp.where(hit, jnp.ones((), BF), jnp.zeros((), BF))


def count_places(wires_ref, fields, hots, counts, upper):
    refs = wires_ref[...]
    usable = refs >= 0
    wire = jnp.where(usable, refs, 0)
    apa = ((wire >> 9) * 205) >> 10
    wire = wire - apa * W
    band = ((wire >> 7) * 205) >> 10
    wire = wire - band * WIRES
    column = (wire * 1639) >> 16
    wire = wire - column * COLS
    pair = wire >> 1
    part = jnp.where(pair >= COLS // 4, 1, 0)
    row = (apa & 1) * WIRES + part * (WIRES // 2) + (wire & 1) * (WIRES // 4)
    row = row + (pair - part * (COLS // 4)) * 16 + column
    source = jnp.where(usable, (apa >> 1) * BANDS + band, 255).astype(F32)
    fields[0:PLACES, :] = ((row >> 7) + 1).astype(F32)
    fields[16 : 16 + PLACES, :] = (row & 127).astype(F32)
    block = BLOBS // 3
    upper[0 : 2 * block, :] = jnp.ones((2 * block, block), BF)
    upper[2 * block :, :] = (
        (iota((block, block), 0) < iota((block, block), 1)).astype(F32).astype(BF)
    )
    group = iota((GROUPS, BLOBS), 0).astype(F32).astype(BF)
    for k in range(PLACES):
        hots[k * GROUPS : (k + 1) * GROUPS, :] = one_if(group == tall(source[k : k + 1], GROUPS))
    for j in range(3):
        counts[:, j * block : (j + 1) * block] = dot(
            hots[:, 0 : (j + 1) * block], upper[(2 - j) * block :, :]
        )


def make_requests(fields, request, bslot, hots, counts):
    blob = iota((1, BLOBS), 1)
    blob_high = ((blob >> 7) + 1).astype(F32)
    blob_low = tall((blob & 127).astype(F32), GROUPS)
    slot = iota((SLOTS, BLOBS), 0).astype(F32).astype(BF)
    before = jnp.zeros((GROUPS, 1), F32)
    all_values = []
    slot_hots = []
    for k in range(PLACES):
        here = slice(k * GROUPS, (k + 1) * GROUPS)
        hot = hots[here, :]
        hot32 = hot.astype(F32)
        count = counts[here, :]
        rank = jnp.sum(hot32 * (count + before), axis=0, keepdims=True)
        before = before + (count + hot32)[:, BLOBS - 1 : BLOBS]
        slot_hots.append(one_if(slot == tall(rank, SLOTS)))
        values = jnp.concatenate(
            [
                hot * tall(fields[k : k + 1, :] * 8.0 + blob_high, GROUPS),
                hot * tall(fields[16 + k : 17 + k, :], GROUPS),
                hot * blob_low,
            ],
            axis=0,
        )
        all_values.append(values)
    table = lax.dot_general(
        jnp.concatenate(all_values, axis=1),
        jnp.concatenate(slot_hots, axis=1),
        (((1,), (1,)), ((), ())),
        preferred_element_type=F32,
    )
    both = table[0:GROUPS].astype(jnp.int32)
    row_high = (both >> 3).astype(F32)
    request[...] = jnp.transpose(
        jnp.concatenate([row_high, table[GROUPS : 2 * GROUPS]], axis=0)
    ).astype(BF)
    bslot[0:GROUPS, :] = (both & 7).astype(F32)
    bslot[GROUPS:, :] = table[2 * GROUPS :]


def pick(reqbox, held, picks, slot, plane, core, band):
    group = plane * 8 + core * BANDS + band
    index = iota((LANES, 2 * LANES), 0)
    choose = index == jnp.where(iota((LANES, 2 * LANES), 1) < LANES, group, group + GROUPS)
    choose = choose.astype(F32).astype(BF)
    height = PICK_OWNERS * SLOTS
    lane = iota((height, LANES), 1).astype(F32).astype(BF)

    def one(n, carry):
        at = pl.ds(PICK_OWNERS * n, PICK_OWNERS)
        asked = reqbox[at].reshape(height, LANES)
        wide = dot(asked, choose)
        high = wide[:, 0:LANES].astype(BF)
        low = one_if(wide[:, LANES:].astype(BF) == lane)
        tiles = [
            jnp.where(high == jnp.asarray(t + 1, BF), low, jnp.zeros((), BF))
            for t in range(2 * WIRES // LANES)
        ]
        got = dot(jnp.concatenate(tiles, axis=1), held[slot])
        picks[slot, at] = got.astype(BF).reshape(PICK_OWNERS, SLOTS, SLICES)
        return carry

    lax.fori_loop(0, PEERS // PICK_OWNERS, one, 0)


def place(bslot, picks, inbox, total, slot, plane, core, band):
    highs = []
    lows = []
    blocks = []
    blob = iota((SLOTS, LANES), 0).astype(F32).astype(BF)
    for r in range(PEERS):
        dc, dy = divmod(r, BANDS)
        from_core = lax.rem(core + dc, 2)
        from_band = lax.rem(band + BANDS - dy, BANDS)
        group = plane * 8 + from_core * BANDS + from_band
        highs.append(tall(bslot[pl.ds(group, 1), :], SLOTS))
        lows.append(one_if(blob == tall(bslot[pl.ds(group + GROUPS, 1), :], SLOTS)))
        blocks.append(picks[slot, 0] if r == 0 else inbox[slot, r])
    incoming = jnp.concatenate(blocks, axis=0)
    high = jnp.concatenate(highs, axis=1)
    low = jnp.concatenate(lows, axis=1)
    hot = jnp.concatenate(
        [
            jnp.where(high == jnp.asarray(m + 1, BF), low, jnp.zeros((), BF))
            for m in range(BLOBS // LANES)
        ],
        axis=0,
    )
    total[...] = total[...] + dot(hot, incoming)


def whole(
    raw_ref, mask_ref, k_ref, wires_ref, sig_ref, blob_ref,
    mask_v, k_v, wires_v, clean, xf, xi, tab, k32, mask8, so, waves, pair_sum, sig_v, held, fields, hots, counts, upper, request, bslot,
    reqbox, picks, inbox,
    halo_send, halo_recv, req_send, req_recv, ring_send, ring_recv, box_send, box_recv, out_sem,
):
    raw_v = sig_v
    fetches = [
        pltpu.make_async_copy(mask_ref, mask_v, out_sem.at[2]),
        pltpu.make_async_copy(raw_ref.at[0], raw_v.at[0], out_sem.at[3]),
        pltpu.make_async_copy(raw_ref.at[1], raw_v.at[1], out_sem.at[4]),
        pltpu.make_async_copy(k_ref, k_v, out_sem.at[5]),
        pltpu.make_async_copy(wires_ref, wires_v, out_sem.at[6]),
    ]
    for fetch in fetches:
        fetch.start()
    apa = lax.axis_index("apa")
    slab = lax.axis_index("slab")
    band = lax.axis_index("band")
    plane = lax.div(apa, 2)
    core = lax.rem(apa, 2)

    def device(dz=0, dc=0, dx=0, dy=0):
        z = lax.rem(plane + dz + PLANES, PLANES)
        c = lax.rem(core + dc, 2)
        return (z * 2 + c, lax.rem(slab + dx + SLABS, SLABS), lax.rem(band + dy + BANDS, BANDS))

    peers = [device(dc=r // BANDS, dy=r % BANDS) for r in range(PEERS)]
    everyone = peers[1:] + [device(dz=1), device(dz=-1), device(dx=1), device(dx=-1)]
    everyone += [device(dx=i, dy=j) for i in (-1, 1) for j in (-1, 1)]
    barrier = pltpu.get_barrier_semaphore()
    for other in everyone:
        pl.semaphore_signal(barrier, inc=1, device_id=other, device_id_type=MESH)

    mask8[...] = jnp.zeros_like(mask8)
    fetches[0].wait()
    mask8[0:2, :] = mask_v[...].astype(F32)
    live = jnp.transpose(mask8[...])

    def remote(src, dst, send, recv, to):
        return pltpu.make_async_remote_copy(
            src_ref=src, dst_ref=dst, send_sem=send, recv_sem=recv, device_id=to, device_id_type=MESH
        )

    own = slice(EDGE, EDGE + WIRES)
    mid = slice(H, H + TICKS)
    row_parts = {
        -1: (slice(EDGE, 2 * EDGE), slice(EDGE + WIRES, TALL)),
        0: (own, own),
        1: (slice(WIRES, EDGE + WIRES), slice(0, EDGE)),
    }
    col_parts = {
        -1: (slice(H, 2 * H), slice(H + TICKS, LONG)),
        0: (mid, mid),
        1: (slice(2 * H, 3 * H), slice(0, H)),
    }
    halos = {0: [], 1: []}
    number = 0
    for ap in range(2):
        fetches[1 + ap].wait()
        mask_waves(raw_v, live, clean, ap)
        if ap == 0:
            fetches[3].wait()
            build_tables(k_v, k32, tab)
            pl.semaphore_wait(barrier, len(everyone))
        for dx in (-1, 1, 0):
            for dy in (-1, 0, 1):
                if dx == 0 and dy == 0:
                    continue
                (rs, rd), (cs, cd) = row_parts[dy], col_parts[dx]
                copy = remote(
                    clean.at[ap, rs, cs], clean.at[ap, rd, cd],
                    halo_send.at[number], halo_recv.at[number], device(dx=dx, dy=dy),
                )
                copy.start()
                halos[ap].append(copy)
                number += 1

    pair_hit = (iota((TICKS, SLICES), 0) >> 1) == iota((TICKS, SLICES), 1)
    pair_sum[...] = pair_hit.astype(F32).astype(BF)
    fetches[4].wait()
    count_places(wires_v, fields, hots, counts, upper)
    make_requests(fields, request, bslot, hots, counts)
    reqbox[0] = request[...]
    asks = []
    for r in range(1, PEERS):
        dc, dy = divmod(r, BANDS)
        back = dc * BANDS + (BANDS - dy) % BANDS
        copy = remote(request, reqbox.at[back], req_send.at[back], req_recv.at[back], peers[r])
        copy.start()
        asks.append(copy)
    has = (slab > 0, slab < SLABS - 1, band > 0, band < BANDS - 1)

    towards = (device(dz=1), device(dz=-1))
    quarter = WIRES // PARTS

    def slot_at(way, distance):
        if distance == 0:
            return 0
        if distance == 4:
            return 7
        return distance + 3 * way

    def ring(way, distance, piece):
        if distance == 1:
            number, rows = piece, slice(piece * quarter, (piece + 1) * quarter)
        else:
            number = 4 + 2 * (distance - 2) + (piece if distance < 4 else 0)
            rows = slice(piece * WIRES, (piece + 1) * WIRES)
        return remote(
            held.at[slot_at(way, distance - 1), rows],
            held.at[slot_at(way, distance), rows],
            ring_send.at[way, number], ring_recv.at[way, number], towards[way],
        )

    writes = []
    started = []
    def start(copy):
        copy.start()
        started.append(copy)

    def forward(distance, half):
        for way in range(2):
            if distance == 1:
                for part in range(PARTS):
                    ring(way, 1, half * PARTS + part).wait_recv()
            else:
                ring(way, distance, half).wait_recv()
            if distance < 3 or half == way:
                start(ring(way, distance + 1, half))

    def receive(ap):
        for copy in halos[ap]:
            copy.wait_recv()
        interleave(clean, xf, xi, ap, has)

    def advance(ap, part):
        convolve(xi, tab, so.at[ap], waves, held, pair_sum, ap, part)
        for way in range(2):
            start(ring(way, 1, ap * PARTS + part))

    receive(0)
    advance(0, 0)
    advance(0, 1)
    receive(1)
    advance(1, 0)
    advance(1, 1)

    def write_signal(ap):
        sig_v[ap] = jnp.concatenate([so[ap, t] for t in range(TICKS // LANES)], axis=1).astype(BF)
        write = pltpu.make_async_copy(sig_v.at[ap], sig_ref.at[ap], out_sem.at[ap])
        write.start()
        writes.append(write)

    boxes = {}

    def serve(slot, shift):
        source = lax.rem(plane + shift + PLANES, PLANES)
        pick(reqbox, held, picks, slot, source, core, band)
        boxes[slot] = []
        for r in (2, 6, 1, 3, 5, 7, 4):
            copy = remote(
                picks.at[slot, r], inbox.at[slot, r], box_send.at[slot, r], box_recv.at[slot, r], peers[r]
            )
            copy.start()
            boxes[slot].append(copy)

    def collect(slot, shift):
        source = lax.rem(plane + shift + PLANES, PLANES)
        for copy in boxes[slot]:
            copy.wait_recv()
        place(bslot, picks, inbox, blob_ref, slot, source, core, band)

    forward(1, 0)
    for copy in asks:
        copy.wait_recv()
    serve(0, 0)
    forward(1, 1)
    serve(1, -1)
    serve(4, 1)
    write_signal(0)
    forward(2, 0)
    write_signal(1)
    blob_ref[...] = jnp.zeros_like(blob_ref)
    collect(0, 0)
    forward(2, 1)
    serve(2, -2)
    serve(5, 2)
    collect(1, -1)
    collect(4, 1)
    forward(3, 0)
    forward(3, 1)
    serve(3, -3)
    serve(6, 3)
    collect(2, -2)
    ring(0, 4, 0).wait_recv()
    ring(1, 4, 1).wait_recv()
    serve(7, 4)
    collect(5, 2)
    collect(3, -3)
    collect(6, 3)
    collect(7, 4)

    for copies in (halos[0], halos[1], asks, started, *boxes.values()):
        for copy in copies:
            copy.wait_send()
    for write in writes:
        write.wait()


def hand_over(signal, charge):
    def body(signal_in, charge_in, signal_out, charge_out):
        signal_out[...] = signal_in[...]
        charge_out[...] = charge_in[...]

    steps = 2
    wave = pl.BlockSpec((2 // steps, WIRES, TICKS), lambda i: (i, 0, 0))
    blob = pl.BlockSpec((BLOBS // steps, SLICES), lambda i: (i, 0))
    return pl.pallas_call(
        body,
        grid=(steps,),
        out_shape=tuple(jax.ShapeDtypeStruct(x.shape, x.dtype) for x in (signal, charge)),
        in_specs=[wave, blob],
        out_specs=(wave, blob),
    )(signal, charge)


def shards(raw, dead_mask, kernel, blob_wires):
    vmem = pl.BlockSpec(memory_space=pltpu.VMEM)
    dma = pltpu.SemaphoreType.DMA
    signal, charge = pl.pallas_call(
        whole,
        out_shape=(
            jax.ShapeDtypeStruct((2, WIRES, TICKS), BF),
            jax.ShapeDtypeStruct((BLOBS, SLICES), F32),
        ),
        in_specs=[pl.BlockSpec(memory_space=pl.ANY)] * 4,
        out_specs=(pl.BlockSpec(memory_space=pl.ANY), vmem),
        scratch_shapes=[
            pltpu.VMEM((2, WIRES), jnp.int32),
            pltpu.VMEM((TAPS, TICKS + 1), BF),
            pltpu.VMEM((PLACES, BLOBS), jnp.int32),
            pltpu.VMEM((2, TALL, LONG), BF),
            pltpu.VMEM((LONG // LANES, TALL, LANES), F32),
            pltpu.VMEM((2, COLS // 2 + WR, 2, 2, 16, REACH), BF),
            pltpu.VMEM((TAPS + 1, REACH, TICKS), BF),
            pltpu.VMEM((24, LONG), F32),
            pltpu.VMEM((8, WIRES), F32),
            pltpu.VMEM((2, TICKS // LANES, WIRES, LANES), F32),
            pltpu.VMEM((WIRES // PARTS, TICKS), BF),
            pltpu.VMEM((TICKS, SLICES), BF),
            pltpu.VMEM((2, WIRES, TICKS), BF),
            pltpu.VMEM((PLANES, 2 * WIRES, SLICES), BF),
            pltpu.VMEM((32, BLOBS), F32),
            pltpu.VMEM((PLACES * GROUPS, BLOBS), BF),
            pltpu.VMEM((PLACES * GROUPS, BLOBS), F32),
            pltpu.VMEM((BLOBS, BLOBS // 3), BF),
            pltpu.VMEM((SLOTS, LANES), BF),
            pltpu.VMEM((LANES, SLOTS), F32),
            pltpu.VMEM((PEERS, SLOTS, LANES), BF),
            pltpu.VMEM((PLANES, PEERS, SLOTS, SLICES), BF),
            pltpu.VMEM((PLANES, PEERS, SLOTS, SLICES), BF),
            dma((16,)),
            dma((16,)),
            dma((PEERS,)),
            dma((PEERS,)),
            dma((2, 9)),
            dma((2, 9)),
            dma((PLANES, PEERS)),
            dma((PLANES, PEERS)),
            dma((7,)),
        ],
        compiler_params=pltpu.CompilerParams(
            collective_id=0, has_side_effects=True, vmem_limit_bytes=56 << 20
        ),
    )(raw, dead_mask, kernel, blob_wires.T)
    return hand_over(signal, charge)


def solution(mesh):
    return jax.shard_map(
        shards,
        mesh=mesh,
        in_specs=(P("apa", "band", "slab"), P("apa", "band"), P(), P(("apa", "band"), None)),
        out_specs=(P("apa", "band", "slab"), P(("apa", "band"), "slab")),
        check_vma=False,
    )
```
